256 devices in a mesh: frame: 16 (over z, core), row: 16 (over x, y).
Axes of the slice: x: 4, y: 4, z: 8, core: 2. Of those that a mesh axis runs over, the one named last changes fastest.
Arguments:
- video_frames: bfloat16 [32, 2048, 2048], P('frame', 'row'), may hold values from -6 to 6
- split_frames: bfloat16 [32, 2048, 2048], P('frame', 'row'), may hold values from -6 to 6
- dual_frames: bfloat16 [32, 2048, 2048], P('frame', 'row'), may hold values from -6 to 6
- sensor_image: float32 [2048, 2048], P('row'), may hold values from -24 to 24
- kernel_vertical: bfloat16 [2, 768], replicated, may hold values from -0.21875 to 0.21875
- kernel_horizontal: bfloat16 [2, 768], replicated, may hold values from -0.21875 to 0.21875
- shutter_start: int32 [16], replicated, may hold values from 0 to 31, as said below
- shutter_end: int32 [16], replicated, may hold values from 1 to 32
Outputs:
- video_next: bfloat16 [32, 2048, 2048], P('frame', 'row')
- split_next: bfloat16 [32, 2048, 2048], P('frame', 'row')
- dual_next: bfloat16 [32, 2048, 2048], P('frame', 'row')
The draws below stay inside these ranges and needn't reach their ends.
Inputs may be any that keep to these rules, and one draw needn't show every extreme that they name: For every row band j, shutter_start[j] < shutter_end[j]; row band j holds sensor rows j * 128 to (j + 1) * 128 - 1.
All inputs are finite; a program needn't handle non-finite values.
Results may differ from the reference program's by a relative error of at most 0.0095.
Values may be sent and summed in bfloat16 or wider, within the bound.
A program may use at most 64 MiB of HBM per device.

```python
import jax
import jax.numpy as jnp
from jax import lax

BLOCK = 128
WIDTH = 2048
RANK = 2
TAPS = 768
FRAMES = 32
HEIGHT = 2048
BANDS = 16


def shutter_pair(key):
    first_draw = jax.random.randint(jax.random.fold_in(key, 1), (BANDS,), 0, FRAMES, dtype=jnp.int32)
    second_draw = jax.random.randint(jax.random.fold_in(key, 2), (BANDS,), 1, FRAMES + 1, dtype=jnp.int32)
    start_value = jnp.minimum(first_draw, second_draw - 1)
    end_value = jnp.maximum(first_draw + 1, second_draw)
    order = jax.random.permutation(jax.random.fold_in(key, 3), BANDS)
    positions = jnp.arange(BANDS, dtype=jnp.int32)
    start_value = jnp.where(positions == order[0], 0, start_value)
    end_value = jnp.where(positions == order[0], 1, end_value)
    start_value = jnp.where(positions == order[1], FRAMES - 1, start_value)
    end_value = jnp.where(positions == order[1], FRAMES, end_value)
    return (start_value.astype(jnp.int32), end_value.astype(jnp.int32))


def draw_shutter_start(key, part):
    return shutter_pair(key)[0]


def draw_shutter_end(key, part):
    return shutter_pair(key)[1]


def shard_levels(own_key, dims, split, low, top_value):
    level = 1.0
    for position, blocks in split:
        steps = jax.random.uniform(jax.random.fold_in(jax.random.fold_in(own_key, 6), position), (blocks,), jnp.float32, low / len(split), top_value / len(split))
        level = level * jnp.repeat(jnp.exp(steps), dims[position] // blocks).reshape((-1,) + (1,) * (len(dims) - 1 - position))
    return level


def centred(rng, shape, deviation, most, cuts=(), held_as=jnp.bfloat16):
    result = jax.random.normal(rng, shape, jnp.float32) * deviation
    if len(cuts) > 0:
        result = shard_levels(rng, shape, cuts, -0.22, 0.18) * result
    return jnp.clip(result, min=-most, max=most).astype(held_as)


def setup_inputs(seed: int = 0) -> dict:
    key_of = jax.random.split(jax.random.key(seed), 9)
    return {
        "video_frames": centred(key_of[0], (FRAMES, HEIGHT, WIDTH), 1.0, 6.0, ((0, 16), (1, 16))),
        "split_frames": centred(key_of[1], (FRAMES, HEIGHT, WIDTH), 1.0, 6.0, ((0, 16), (1, 16))),
        "dual_frames": centred(key_of[2], (FRAMES, HEIGHT, WIDTH), 1.0, 6.0, ((0, 16), (1, 16))),
        "sensor_image": centred(key_of[3], (HEIGHT, WIDTH), 4.0, 24.0, ((0, 16),), jnp.float32),
        "kernel_vertical": centred(key_of[4], (RANK, TAPS), TAPS ** -0.5, 0.21875),
        "kernel_horizontal": centred(key_of[5], (RANK, TAPS), TAPS ** -0.5, 0.21875),
        "shutter_start": draw_shutter_start(jax.random.fold_in(key_of[8], 71), 0),
        "shutter_end": draw_shutter_end(jax.random.fold_in(key_of[8], 71), 0),
    }


tau_step = 0.1
rho_weight = 2.0


def toeplitz_blocks(kernel, block_rows):
    rank_count = kernel.shape[0]
    padded = jnp.pad(kernel, ((0, 0), (block_rows, block_rows)))
    pieces = jnp.stack([padded[:, block_rows * e + 1:block_rows * e + 2 * block_rows] for e in range(7)], axis=1)
    wrapped = jnp.pad(pieces, ((0, 0), (0, 0), (0, 1)))
    tiled = jnp.tile(wrapped, (1, 1, block_rows))
    shaped = tiled[:, :, :block_rows * (2 * block_rows - 1)].reshape(rank_count, 7, block_rows, 2 * block_rows - 1)
    return shaped[:, :, :, block_rows - 1:2 * block_rows - 1]


def rows_pass(blocks, frame, adjoint):
    height, width_cols = frame.shape
    margin = 3 * BLOCK
    padded = jnp.pad(frame, ((margin, margin), (0, 0)))
    pattern = "rji,pjw->rpiw" if adjoint else "rij,pjw->rpiw"
    summed = jnp.zeros((RANK, height // BLOCK, BLOCK, width_cols), jnp.float32)
    for offset in range(-3, 4):
        begin_row = (3 - offset if adjoint else 3 + offset) * BLOCK
        row_view = padded[begin_row:begin_row + height].reshape(height // BLOCK, BLOCK, width_cols)
        summed = summed + jnp.einsum(pattern, blocks[:, offset + 3].astype(jnp.float32), row_view.astype(jnp.float32))
    return summed.reshape(RANK, height, width_cols)


def columns_pass(blocks, data, adjoint):
    rank_count, row_count, width_cols = data.shape
    margin = 3 * BLOCK
    padded = jnp.pad(data, ((0, 0), (0, 0), (margin, margin)))
    pattern = "rhnj,rji->hni" if adjoint else "rhnj,rij->hni"
    summed = jnp.zeros((row_count, width_cols // BLOCK, BLOCK), jnp.float32)
    for offset in range(-3, 4):
        begin_col = (3 - offset if adjoint else 3 + offset) * BLOCK
        col_view = padded[:, :, begin_col:begin_col + width_cols].reshape(rank_count, row_count, width_cols // BLOCK, BLOCK)
        summed = summed + jnp.einsum(pattern, col_view.astype(jnp.float32), blocks[:, offset + 3].astype(jnp.float32))
    return summed.reshape(row_count, width_cols)


def reference(video_frames, split_frames, dual_frames, sensor_image, kernel_vertical, kernel_horizontal, shutter_start, shutter_end):
    vertical_blocks = toeplitz_blocks(kernel_vertical, BLOCK)
    horizontal_blocks = toeplitz_blocks(kernel_horizontal, BLOCK)
    band_rows = jnp.arange(HEIGHT, dtype=jnp.int32) // BLOCK
    start_rows = shutter_start[band_rows]
    end_rows = shutter_end[band_rows]

    def active_rows(frame_index):
        return (start_rows <= frame_index) & (frame_index < end_rows)

    def accumulate(measured, item):
        frame_index, frame = item
        rowed = rows_pass(vertical_blocks, frame, False).astype(jnp.bfloat16)
        blurred = columns_pass(horizontal_blocks, rowed, False).astype(jnp.bfloat16)
        measured = measured + jnp.where(active_rows(frame_index)[:, None], blurred.astype(jnp.float32), jnp.zeros((), jnp.float32))
        return measured, None

    frame_ids = jnp.arange(FRAMES, dtype=jnp.int32)
    measured, _ = lax.scan(accumulate, jnp.zeros((HEIGHT, WIDTH), jnp.float32), (frame_ids, video_frames))
    residual = (measured - sensor_image).astype(jnp.bfloat16)

    def update(item):
        frame_index, frame, split_frame, dual_frame = item
        masked = jnp.where(active_rows(frame_index)[:, None], residual, jnp.zeros((), jnp.bfloat16))
        back = rows_pass(vertical_blocks, masked, True).astype(jnp.bfloat16)
        gradient = columns_pass(horizontal_blocks, back, True)
        current = frame.astype(jnp.float32)
        dual_value = dual_frame.astype(jnp.float32)
        moved_frames = current - tau_step * (gradient + rho_weight * (current - split_frame.astype(jnp.float32) + dual_value))
        shifted = moved_frames + dual_value
        clamped = jnp.maximum(shifted, 0.0)
        return moved_frames.astype(jnp.bfloat16), clamped.astype(jnp.bfloat16), (shifted - clamped).astype(jnp.bfloat16)

    video_next, split_next, dual_next = lax.map(update, (frame_ids, video_frames, split_frames, dual_frames))
    return (video_next, split_next, dual_next)
```

```python
import functools

import jax
import jax.numpy as jnp
from jax import lax
from jax.experimental import pallas as pl
from jax.experimental.pallas import tpu as pltpu
from jax.sharding import PartitionSpec as P

MESH = pl.DeviceIdType.MESH
tau_step = 0.1
rho_weight = 2.0
REACH = 3
DIAGS = 2 * REACH + 1
F32 = jnp.float32
BF16 = jnp.bfloat16


def dot(a, b, contract):
    return lax.dot_general(a, b, (contract, ((), ())), preferred_element_type=F32)


def wrap(index, count):
    return lax.rem(index + count, count)


def banded(kernel_ref, out_ref, block):
    rank_count, taps = kernel_ref.shape
    padded = jnp.concatenate(
        [kernel_ref[...].astype(F32), jnp.zeros((rank_count, block), F32)], axis=1
    )
    for r in range(rank_count):
        rows = jnp.broadcast_to(padded[r : r + 1], (block, taps + block))
        out_ref[r] = pltpu.roll(rows, 0, 1, stride=1, stride_axis=0).astype(BF16)


def kernel(
    start_ref, end_ref, video_ref, sensor_ref, kv_ref, kh_ref, grad_ref,
    frames_buf, sensor_buf, vert, horiz, sums, t_send, t_recv, p_send, p_recv, res_recv, h_send, h_recv, g_send,
    local_sem, a_send, a_recv, ts_sem, tr_sem, ps_sem, pr_sem, rs_sem, rr_sem, hs_sem, hr_sem, gs_sem, gr_sem,
):
    frame_devices, local_count, block, slice_cols = frames_buf.shape
    bands = start_ref.shape[0]
    rank_count = kv_ref.shape[0]
    me = lax.axis_index("frame")
    band = lax.axis_index("row")
    steps = [d for d in range(-REACH, REACH + 1) if d != 0]

    def frame_peer(d):
        return (wrap(me + d, frame_devices), band)

    def row_peer(d):
        return (me, wrap(band + d, bands))

    def columns(index):
        return pl.ds(pl.multiple_of(index * slice_cols, slice_cols), slice_cols)

    barrier = pltpu.get_barrier_semaphore()

    def greet(k, carry):
        pl.semaphore_signal(barrier, inc=1, device_id=frame_peer(k), device_id_type=MESH)
        return carry

    lax.fori_loop(1, frame_devices, greet, 0)
    for d in steps:
        pl.semaphore_signal(barrier, inc=1, device_id=row_peer(d), device_id_type=MESH)
    pl.semaphore_wait(barrier, frame_devices - 1 + len(steps))

    def a_copy(k):
        target = frame_peer(k)
        return pltpu.make_async_remote_copy(
            src_ref=video_ref.at[:, :, columns(target[0])],
            dst_ref=frames_buf.at[me],
            send_sem=a_send.at[k],
            recv_sem=a_recv.at[k],
            device_id=target,
            device_id_type=MESH,
        )

    def start_a(k, carry):
        a_copy(k).start()
        return carry

    lax.fori_loop(1, frame_devices, start_a, 0)
    own_copy = pltpu.make_async_copy(
        video_ref.at[:, :, columns(me)], frames_buf.at[me], local_sem.at[0]
    )
    own_copy.start()
    sensor_copy = pltpu.make_async_copy(sensor_ref.at[:, columns(me)], sensor_buf, local_sem.at[1])
    sensor_copy.start()

    banded(kv_ref, vert, block)
    banded(kh_ref, horiz, block)

    def on(frame, band_index):
        inside = (band_index >= 0) & (band_index < bands)
        at = jnp.clip(band_index, 0, bands - 1)
        active = inside & (start_ref[at] <= frame) & (frame < end_ref[at])
        return jnp.where(active, 1.0, 0.0).astype(F32)

    def add_frames(source, first):
        for d in range(-REACH, REACH + 1):
            total = None if first else sums[d + REACH]
            for i in range(local_count):
                term = frames_buf[source, i].astype(F32) * on(source * local_count + i, band + d)
                total = term if total is None else total + term
            sums[d + REACH] = total

    own_copy.wait()
    add_frames(me, True)

    def arrive(k, carry):
        a_copy(k).wait_recv()
        add_frames(wrap(me - k, frame_devices), False)
        return carry

    lax.fori_loop(1, frame_devices, arrive, 0)

    def send(src, dst, send_sem, recv_sem, target):
        copy = pltpu.make_async_remote_copy(
            src_ref=src, dst_ref=dst, send_sem=send_sem, recv_sem=recv_sem,
            device_id=target, device_id_type=MESH,
        )
        copy.start()
        return copy

    def kept(value, index, count):
        return value * jnp.where((index >= 0) & (index < count), 1.0, 0.0).astype(value.dtype)

    t_copies = []
    for d in steps:
        t_send[d + REACH] = sums[d + REACH].astype(BF16)
        t_copies.append(
            send(t_send.at[d + REACH], t_recv.at[REACH - d], ts_sem.at[d + REACH], tr_sem.at[REACH - d], row_peer(d))
        )
    t_recv[REACH] = sums[REACH].astype(BF16)
    for copy in t_copies:
        copy.wait()
    window = jnp.concatenate(
        [kept(t_recv[d + REACH], band + d, bands) for d in range(-REACH, REACH + 1)], axis=0
    )
    rowed = [dot(vert[r], window, ((1,), (0,))).astype(BF16) for r in range(rank_count)]

    def part(d):
        total = None
        for r in range(rank_count):
            block_d = horiz[r, :, (d + REACH) * block : (d + REACH + 1) * block]
            term = dot(rowed[r], block_d, ((1,), (1,)))
            total = term if total is None else total + term
        return total

    p_copies = []
    for d in steps:
        p_send[d + REACH] = part(d).astype(BF16)
        p_copies.append(
            send(p_send.at[d + REACH], p_recv.at[d + REACH], ps_sem.at[d + REACH], pr_sem.at[d + REACH], frame_peer(-d))
        )
    measured = part(0)
    for copy in p_copies:
        copy.wait()
    for d in steps:
        measured = measured + kept(p_recv[d + REACH].astype(F32), me + d, frame_devices)
    sensor_copy.wait()
    residual = (measured - sensor_buf[...]).astype(BF16)

    res_recv[REACH] = residual
    r_copies = [
        send(res_recv.at[REACH], res_recv.at[d + REACH], rs_sem.at[d + REACH], rr_sem.at[d + REACH], frame_peer(d))
        for d in steps
    ]
    for copy in r_copies:
        copy.wait()
    pieces = [kept(res_recv[d + REACH], me - d, frame_devices) for d in range(-REACH, REACH + 1)]
    spread = []
    for r in range(rank_count):
        total = None
        for d in range(-REACH, REACH + 1):
            block_d = horiz[r, :, (d + REACH) * block : (d + REACH + 1) * block]
            term = dot(pieces[d + REACH], block_d, ((1,), (0,)))
            total = term if total is None else total + term
        spread.append(total.astype(BF16))

    def back(d):
        total = None
        for r in range(rank_count):
            block_d = vert[r, :, (d + REACH) * block : (d + REACH + 1) * block]
            term = dot(block_d, spread[r], ((0,), (0,)))
            total = term if total is None else total + term
        return total.astype(BF16)

    h_copies = []
    for d in steps:
        h_send[d + REACH] = back(d)
        h_copies.append(
            send(h_send.at[d + REACH], h_recv.at[d + REACH], hs_sem.at[d + REACH], hr_sem.at[d + REACH], row_peer(d))
        )
    h_recv[REACH] = back(0)
    for copy in h_copies:
        copy.wait()

    def gradients(target):
        for i in range(local_count):
            total = None
            for d in range(-REACH, REACH + 1):
                term = h_recv[d + REACH].astype(F32) * on(target * local_count + i, band - d)
                total = term if total is None else total + term
            g_send[target, i] = total.astype(BF16)

    def g_copy(k):
        target = frame_peer(k)
        return pltpu.make_async_remote_copy(
            src_ref=g_send.at[target[0]],
            dst_ref=grad_ref.at[:, :, columns(me)],
            send_sem=gs_sem.at[k],
            recv_sem=gr_sem.at[k],
            device_id=target,
            device_id_type=MESH,
        )

    def give(k, carry):
        gradients(wrap(me + k, frame_devices))
        g_copy(k).start()
        return carry

    lax.fori_loop(1, frame_devices, give, 0)
    gradients(me)
    own_grad = pltpu.make_async_copy(g_send.at[me], grad_ref.at[:, :, columns(me)], local_sem.at[0])
    own_grad.start()

    def finish(k, carry):
        a_copy(k).wait_send()
        g_copy(k).wait()
        return carry

    lax.fori_loop(1, frame_devices, finish, 0)
    own_grad.wait()


def per_device(
    video_frames, split_frames, dual_frames, sensor_image, kernel_vertical, kernel_horizontal, shutter_start, shutter_end
):
    local_count, block, width = video_frames.shape
    rank_count, taps = kernel_vertical.shape
    frame_devices = lax.axis_size("frame")
    slice_cols = width // frame_devices
    smem = pl.BlockSpec(memory_space=pltpu.SMEM)
    vmem = pl.BlockSpec(memory_space=pltpu.VMEM)
    anywhere = pl.BlockSpec(memory_space=pl.ANY)
    dma = pltpu.SemaphoreType.DMA
    tile = (block, slice_cols)
    gradient = pl.pallas_call(
        kernel,
        out_shape=jax.ShapeDtypeStruct((local_count, block, width), BF16),
        in_specs=[smem, smem, anywhere, anywhere, vmem, vmem],
        out_specs=anywhere,
        scratch_shapes=[
            pltpu.VMEM((frame_devices, local_count) + tile, BF16),
            pltpu.VMEM(tile, F32),
            pltpu.VMEM((rank_count, block, taps + block), BF16),
            pltpu.VMEM((rank_count, block, taps + block), BF16),
            pltpu.VMEM((DIAGS,) + tile, F32),
        ]
        + [pltpu.VMEM((DIAGS,) + tile, BF16)] * 7
        + [pltpu.VMEM((frame_devices, local_count) + tile, BF16)]
        + [dma((2,)), dma((frame_devices,)), dma((frame_devices,))]
        + [dma((DIAGS,))] * 8
        + [dma((frame_devices,)), dma((frame_devices,))],
        compiler_params=pltpu.CompilerParams(
            collective_id=0, has_side_effects=True, vmem_limit_bytes=32 << 20
        ),
        name="blur_and_adjoint",
    )(shutter_start, shutter_end, video_frames, sensor_image, kernel_vertical, kernel_horizontal)
    current = video_frames.astype(F32)
    dual_value = dual_frames.astype(F32)
    moved_frames = current - tau_step * (
        gradient.astype(F32) + rho_weight * (current - split_frames.astype(F32) + dual_value)
    )
    shifted = moved_frames + dual_value
    clamped = jnp.maximum(shifted, 0.0)
    return (
        moved_frames.astype(BF16),
        clamped.astype(BF16),
        (shifted - clamped).astype(BF16),
    )


def solution(mesh):
    frames = P("frame", "row", None)
    return jax.shard_map(
        per_device,
        mesh=mesh,
        in_specs=(frames, frames, frames, P("row", None), P(), P(), P(), P()),
        out_specs=(frames, frames, frames),
        check_vma=False,
    )
```

```python
import functools

import jax
import jax.numpy as jnp
from jax import lax
from jax.experimental import pallas as pl
from jax.experimental.pallas import tpu as pltpu
from jax.sharding import PartitionSpec as P

MESH = pl.DeviceIdType.MESH
tau_step = 0.1
rho_weight = 2.0
REACH = 3
DIAGS = 2 * REACH + 1
F32 = jnp.float32
BF16 = jnp.bfloat16


def dot(a, b, contract):
    return lax.dot_general(a, b, (contract, ((), ())), preferred_element_type=F32)


def wrap(index, count):
    return lax.rem(index + count, count)


def banded(kernel_ref, out_ref, block):
    rank_count, taps = kernel_ref.shape
    padded = jnp.concatenate(
        [kernel_ref[...].astype(F32), jnp.zeros((rank_count, block), F32)], axis=1
    )
    for r in range(rank_count):
        rows = jnp.broadcast_to(padded[r : r + 1], (block, taps + block))
        out_ref[r] = pltpu.roll(rows, 0, 1, stride=1, stride_axis=0).astype(BF16)


def kernel(
    start_hbm, end_hbm, video_ref, sensor_ref, kv_hbm, kh_hbm, grad_ref,
    start_ref, end_ref, kv_ref, kh_ref, frames_buf, sensor_buf, vert, horiz, sums, t_send, t_recv, p_send, p_recv, res_recv, h_send, h_recv, g_send,
    local_sem, a_send, a_recv, ts_sem, tr_sem, ps_sem, pr_sem, rs_sem, rr_sem, hs_sem, hr_sem, gs_sem, gr_sem,
):
    frame_devices, local_count, block, slice_cols = frames_buf.shape
    bands = start_ref.shape[0]
    rank_count = kv_ref.shape[0]
    me = lax.axis_index("frame")
    band = lax.axis_index("row")
    steps = [d for d in range(-REACH, REACH + 1) if d != 0]

    def frame_peer(d):
        return (wrap(me + d, frame_devices), band)

    def row_peer(d):
        return (me, wrap(band + d, bands))

    def columns(index):
        return pl.ds(pl.multiple_of(index * slice_cols, slice_cols), slice_cols)

    small = [
        pltpu.make_async_copy(src, dst, local_sem.at[2 + i])
        for i, (src, dst) in enumerate(
            [(start_hbm, start_ref), (end_hbm, end_ref), (kv_hbm, kv_ref), (kh_hbm, kh_ref)]
        )
    ]
    for copy in small:
        copy.start()
    barrier = pltpu.get_barrier_semaphore()

    def greet(k, carry):
        pl.semaphore_signal(barrier, inc=1, device_id=frame_peer(k), device_id_type=MESH)
        return carry

    lax.fori_loop(1, frame_devices, greet, 0)
    for d in steps:
        pl.semaphore_signal(barrier, inc=1, device_id=row_peer(d), device_id_type=MESH)
    pl.semaphore_wait(barrier, frame_devices - 1 + len(steps))

    def a_copy(k):
        target = frame_peer(k)
        return pltpu.make_async_remote_copy(
            src_ref=video_ref.at[:, :, columns(target[0])],
            dst_ref=frames_buf.at[me],
            send_sem=a_send.at[k],
            recv_sem=a_recv.at[k],
            device_id=target,
            device_id_type=MESH,
        )

    def start_a(k, carry):
        a_copy(k).start()
        return carry

    lax.fori_loop(1, frame_devices, start_a, 0)
    own_copy = pltpu.make_async_copy(
        video_ref.at[:, :, columns(me)], frames_buf.at[me], local_sem.at[0]
    )
    own_copy.start()
    sensor_copy = pltpu.make_async_copy(sensor_ref.at[:, columns(me)], sensor_buf, local_sem.at[1])
    sensor_copy.start()
    for copy in small:
        copy.wait()

    banded(kv_ref, vert, block)
    banded(kh_ref, horiz, block)

    def on(frame, band_index):
        inside = (band_index >= 0) & (band_index < bands)
        at = jnp.clip(band_index, 0, bands - 1)
        active = inside & (start_ref[at] <= frame) & (frame < end_ref[at])
        return jnp.where(active, 1.0, 0.0).astype(F32)

    def add_frames(source, first):
        for d in range(-REACH, REACH + 1):
            total = None if first else sums[d + REACH]
            for i in range(local_count):
                term = frames_buf[source, i].astype(F32) * on(source * local_count + i, band + d)
                total = term if total is None else total + term
            sums[d + REACH] = total

    own_copy.wait()
    add_frames(me, True)

    def arrive(k, carry):
        a_copy(k).wait_recv()
        add_frames(wrap(me - k, frame_devices), False)
        return carry

    lax.fori_loop(1, frame_devices, arrive, 0)

    sent = []

    def send(src, dst, send_sem, recv_sem, target):
        copy = pltpu.make_async_remote_copy(
            src_ref=src, dst_ref=dst, send_sem=send_sem, recv_sem=recv_sem,
            device_id=target, device_id_type=MESH,
        )
        copy.start()
        sent.append(copy)
        return copy

    def kept(value, index, count):
        return value * jnp.where((index >= 0) & (index < count), 1.0, 0.0).astype(value.dtype)

    t_copies = []
    for d in steps:
        t_send[d + REACH] = sums[d + REACH].astype(BF16)
        t_copies.append(
            send(t_send.at[d + REACH], t_recv.at[REACH - d], ts_sem.at[d + REACH], tr_sem.at[REACH - d], row_peer(d))
        )
    t_recv[REACH] = sums[REACH].astype(BF16)
    for copy in t_copies:
        copy.wait_recv()
    window = jnp.concatenate(
        [kept(t_recv[d + REACH], band + d, bands) for d in range(-REACH, REACH + 1)], axis=0
    )
    rowed = [dot(vert[r], window, ((1,), (0,))).astype(BF16) for r in range(rank_count)]

    def part(d):
        total = None
        for r in range(rank_count):
            block_d = horiz[r, :, (d + REACH) * block : (d + REACH + 1) * block]
            term = dot(rowed[r], block_d, ((1,), (1,)))
            total = term if total is None else total + term
        return total

    p_copies = []
    for d in steps:
        p_send[d + REACH] = part(d).astype(BF16)
        p_copies.append(
            send(p_send.at[d + REACH], p_recv.at[d + REACH], ps_sem.at[d + REACH], pr_sem.at[d + REACH], frame_peer(-d))
        )
    measured = part(0)
    for copy in p_copies:
        copy.wait_recv()
    for d in steps:
        measured = measured + kept(p_recv[d + REACH].astype(F32), me + d, frame_devices)
    sensor_copy.wait()
    residual = (measured - sensor_buf[...]).astype(BF16)

    res_recv[REACH] = residual
    r_copies = [
        send(res_recv.at[REACH], res_recv.at[d + REACH], rs_sem.at[d + REACH], rr_sem.at[d + REACH], frame_peer(d))
        for d in steps
    ]
    for copy in r_copies:
        copy.wait_recv()
    pieces = [kept(res_recv[d + REACH], me - d, frame_devices) for d in range(-REACH, REACH + 1)]
    spread = []
    for r in range(rank_count):
        total = None
        for d in range(-REACH, REACH + 1):
            block_d = horiz[r, :, (d + REACH) * block : (d + REACH + 1) * block]
            term = dot(pieces[d + REACH], block_d, ((1,), (0,)))
            total = term if total is None else total + term
        spread.append(total.astype(BF16))

    def back(d):
        total = None
        for r in range(rank_count):
            block_d = vert[r, :, (d + REACH) * block : (d + REACH + 1) * block]
            term = dot(block_d, spread[r], ((0,), (0,)))
            total = term if total is None else total + term
        return total.astype(BF16)

    h_copies = []
    for d in steps:
        h_send[d + REACH] = back(d)
        h_copies.append(
            send(h_send.at[d + REACH], h_recv.at[d + REACH], hs_sem.at[d + REACH], hr_sem.at[d + REACH], row_peer(d))
        )
    h_recv[REACH] = back(0)
    for copy in h_copies:
        copy.wait_recv()

    def gradients(target):
        for i in range(local_count):
            total = None
            for d in range(-REACH, REACH + 1):
                term = h_recv[d + REACH].astype(F32) * on(target * local_count + i, band - d)
                total = term if total is None else total + term
            g_send[target, i] = total.astype(BF16)

    def g_copy(k):
        target = frame_peer(k)
        return pltpu.make_async_remote_copy(
            src_ref=g_send.at[target[0]],
            dst_ref=grad_ref.at[:, :, columns(me)],
            send_sem=gs_sem.at[k],
            recv_sem=gr_sem.at[k],
            device_id=target,
            device_id_type=MESH,
        )

    def give(k, carry):
        gradients(wrap(me + k, frame_devices))
        g_copy(k).start()
        return carry

    lax.fori_loop(1, frame_devices, give, 0)
    gradients(me)
    own_grad = pltpu.make_async_copy(g_send.at[me], grad_ref.at[:, :, columns(me)], local_sem.at[0])
    own_grad.start()

    def finish(k, carry):
        a_copy(k).wait_send()
        g_copy(k).wait()
        return carry

    lax.fori_loop(1, frame_devices, finish, 0)
    own_grad.wait()
    for copy in sent:
        copy.wait_send()


def per_device(
    video_frames, split_frames, dual_frames, sensor_image, kernel_vertical, kernel_horizontal, shutter_start, shutter_end
):
    local_count, block, width = video_frames.shape
    rank_count, taps = kernel_vertical.shape
    frame_devices = lax.axis_size("frame")
    slice_cols = width // frame_devices
    hbm = pl.BlockSpec(memory_space=pltpu.HBM)
    anywhere = pl.BlockSpec(memory_space=pl.ANY)
    dma = pltpu.SemaphoreType.DMA
    tile = (block, slice_cols)
    operands = (shutter_start, shutter_end, video_frames, sensor_image, kernel_vertical, kernel_horizontal)
    gradient = pl.pallas_call(
        kernel,
        out_shape=jax.ShapeDtypeStruct((local_count, block, width), BF16),
        in_specs=[hbm] * 6,
        out_specs=anywhere,
        scratch_shapes=[
            pltpu.SMEM(shutter_start.shape, jnp.int32),
            pltpu.SMEM(shutter_end.shape, jnp.int32),
            pltpu.VMEM((rank_count, taps), BF16),
            pltpu.VMEM((rank_count, taps), BF16),
            pltpu.VMEM((frame_devices, local_count) + tile, BF16),
            pltpu.VMEM(tile, F32),
            pltpu.VMEM((rank_count, block, taps + block), BF16),
            pltpu.VMEM((rank_count, block, taps + block), BF16),
            pltpu.VMEM((DIAGS,) + tile, F32),
        ]
        + [pltpu.VMEM((DIAGS,) + tile, BF16)] * 7
        + [pltpu.VMEM((frame_devices, local_count) + tile, BF16)]
        + [dma((6,)), dma((frame_devices,)), dma((frame_devices,))]
        + [dma((DIAGS,))] * 8
        + [dma((frame_devices,)), dma((frame_devices,))],
        compiler_params=pltpu.CompilerParams(
            collective_id=0, has_side_effects=True, vmem_limit_bytes=32 << 20
        ),
        name="blur_and_adjoint",
    )(*[pltpu.with_memory_space_constraint(x, pltpu.HBM) for x in operands])
    current = video_frames.astype(F32)
    dual_value = dual_frames.astype(F32)
    moved_frames = current - tau_step * (
        gradient.astype(F32) + rho_weight * (current - split_frames.astype(F32) + dual_value)
    )
    shifted = moved_frames + dual_value
    clamped = jnp.maximum(shifted, 0.0)
    return (
        moved_frames.astype(BF16),
        clamped.astype(BF16),
        (shifted - clamped).astype(BF16),
    )


def solution(mesh):
    frames = P("frame", "row", None)
    return jax.shard_map(
        per_device,
        mesh=mesh,
        in_specs=(frames, frames, frames, P("row", None), P(), P(), P(), P()),
        out_specs=(frames, frames, frames),
        check_vma=False,
    )
```

```python
import functools

import jax
import jax.numpy as jnp
from jax import lax
from jax.experimental import pallas as pl
from jax.experimental.pallas import tpu as pltpu
from jax.sharding import PartitionSpec as P

MESH = pl.DeviceIdType.MESH
tau_step = 0.1
rho_weight = 2.0
REACH = 3
DIAGS = 2 * REACH + 1
F32 = jnp.float32
BF16 = jnp.bfloat16


def dot(a, b, contract):
    return lax.dot_general(a, b, (contract, ((), ())), preferred_element_type=F32)


def wrap(index, count):
    return lax.rem(index + count, count)


def banded(kernel_ref, out_ref, block):
    rank_count, taps = kernel_ref.shape
    padded = jnp.concatenate(
        [kernel_ref[...].astype(F32), jnp.zeros((rank_count, block), F32)], axis=1
    )
    for r in range(rank_count):
        rows = jnp.broadcast_to(padded[r : r + 1], (block, taps + block))
        out_ref[r] = pltpu.roll(rows, 0, 1, stride=1, stride_axis=0).astype(BF16)


def kernel(
    start_hbm, end_hbm, video_ref, sensor_ref, kv_hbm, kh_hbm, grad_ref,
    start_ref, end_ref, kv_ref, kh_ref, sensor_buf, vert, horiz, sums, rowed_ref, spread,
    frames_buf, own_buf, swap_buf, tb_send, tb_recv, part_send, part_recv, t_send, t_recv,
    p_send, p_recv, res_recv, h_send, h_recv, q_recv, hb_send, hb_recv, g_send, gb_send,
    local_sem, own_sem, sw_s, sw_r, a_s, a_r, tb_s, tb_r, part_s, part_r, t_s, t_r,
    p_s, p_r, r_s, r_r, h_s, h_r, q_s, q_r, hb_s, hb_r, g_s, g_r, gb_s, gb_r,
):
    frame_devices, local_count, block, slice_cols = frames_buf.shape
    chips = frame_devices // 2
    shares = chips // 2
    bands = start_ref.shape[0]
    rank_count = kv_ref.shape[0]
    me = lax.axis_index("frame")
    band = lax.axis_index("row")
    chip = me // 2
    core = lax.rem(me, 2)
    sibling = me + 1 - 2 * core
    skew = lax.rem(core + chip, 2)
    steps = [2, -2, 3, -3, 1, -1]
    diagonals = range(-REACH, REACH + 1)

    def frame_peer(d):
        return (wrap(me + d, frame_devices), band)

    def row_peer(d):
        return (me, wrap(band + d, bands))

    def columns(index):
        return pl.ds(pl.multiple_of(index * slice_cols, slice_cols), slice_cols)

    def odd_chip(i):
        return lax.rem(chip + skew + 2 * i, chips)

    def remote(src, dst, send_sem, recv_sem, target):
        return pltpu.make_async_remote_copy(
            src_ref=src, dst_ref=dst, send_sem=send_sem, recv_sem=recv_sem,
            device_id=target, device_id_type=MESH,
        )

    small = [
        pltpu.make_async_copy(src, dst, local_sem.at[2 + i])
        for i, (src, dst) in enumerate(
            [(start_hbm, start_ref), (end_hbm, end_ref), (kv_hbm, kv_ref), (kh_hbm, kh_ref)]
        )
    ]
    for copy in small:
        copy.start()
    own_copies = [
        pltpu.make_async_copy(video_ref.at[:, :, columns(2 * odd_chip(i) + 1)], own_buf.at[i], own_sem.at[i])
        for i in range(shares)
    ]
    for copy in own_copies:
        copy.start()
    own_even = pltpu.make_async_copy(video_ref.at[:, :, columns(2 * chip)], frames_buf.at[me], local_sem.at[0])
    sensor_copy = pltpu.make_async_copy(sensor_ref.at[:, columns(me)], sensor_buf, local_sem.at[1])
    sensor_copy.start()

    @pl.when(core == 0)
    def _():
        own_even.start()

    barrier = pltpu.get_barrier_semaphore()

    def greet(k, carry):
        pl.semaphore_signal(barrier, inc=1, device_id=frame_peer(k), device_id_type=MESH)
        return carry

    lax.fori_loop(1, frame_devices, greet, 0)
    for d in steps:
        pl.semaphore_signal(barrier, inc=1, device_id=row_peer(d), device_id_type=MESH)
    pl.semaphore_wait(barrier, frame_devices - 1 + len(steps))

    def swap_copy(i):
        index = 2 * lax.rem(chip + 1 - skew + 2 * i, chips) + 1
        return remote(video_ref.at[:, :, columns(index)], swap_buf.at[i], sw_s.at[i], sw_r.at[i], (sibling, band))

    def even_copy(k):
        target = 2 * lax.rem(chip + k, chips)
        return remote(
            video_ref.at[:, :, columns(target)], frames_buf.at[me], a_s.at[k], a_r.at[2 * k + core], (target, band)
        )

    order_b = [2, 1, 3, 0]
    for i in order_b:
        swap_copy(i).start()

    def start_even(k, carry):
        even_copy(k).start()
        return carry

    lax.fori_loop(1, chips, start_even, 0)

    @pl.when(core == 1)
    def _():
        even_copy(0).start()

    for copy in small:
        copy.wait()
    banded(kv_ref, vert, block)
    banded(kh_ref, horiz, block)

    def on(frame, band_index):
        inside = (band_index >= 0) & (band_index < bands)
        at = jnp.clip(band_index, 0, bands - 1)
        active = inside & (start_ref[at] <= frame) & (frame < end_ref[at])
        return jnp.where(active, 1.0, 0.0).astype(F32)

    def kept(value, index, count):
        return value * jnp.where((index >= 0) & (index < count), 1.0, 0.0).astype(value.dtype)

    def weighted(pairs):
        total = None
        for value, weight in pairs:
            total = value * weight if total is None else total + value * weight
        return total

    def tb_copy(i, d):
        return remote(
            tb_send.at[i, d + REACH], tb_recv.at[i, REACH - d], tb_s.at[i, d + REACH], tb_r.at[i, REACH - d], row_peer(d)
        )

    def tb_arrival(i, d):
        return remote(tb_send.at[i, d + REACH], tb_recv.at[i, d + REACH], tb_s.at[i, d + REACH], tb_r.at[i, d + REACH], row_peer(d))

    half = block // 4
    for i in order_b:
        own_copies[i].wait()
        swap_copy(i).wait_recv()

        def mix(c, carry):
            part = pl.ds(pl.multiple_of(c * half, half), half)
            mine = [(own_buf[i, f, part].astype(F32), me * local_count + f) for f in range(local_count)]
            others = [(swap_buf[i, f, part].astype(F32), sibling * local_count + f) for f in range(local_count)]
            for d in diagonals:
                total = weighted([(value, on(frame, band + d)) for value, frame in mine + others]).astype(BF16)
                if d == 0:
                    tb_recv[i, REACH, part] = total
                else:
                    tb_send[i, d + REACH, part] = total
            return carry

        lax.fori_loop(0, 4, mix, 0)
        for d in steps:
            tb_copy(i, d).start()

    def add_frames(source, first):
        for d in diagonals:
            total = None if first else sums[d + REACH]
            for f in range(local_count):
                term = frames_buf[source, f].astype(F32) * on(source * local_count + f, band + d)
                total = term if total is None else total + term
            sums[d + REACH] = total

    def even_arrival(k, from_core):
        source = 2 * wrap(chip - k, chips) + from_core
        remote(frames_buf.at[source], frames_buf.at[source], a_s.at[k], a_r.at[2 * k + from_core], (sibling, band)).wait_recv()
        add_frames(source, False)

    def gather_even(low, high):
        def take(q, carry):
            k = wrap(((q + 1) // 2) * (2 * lax.rem(q, 2) - 1), chips)
            even_arrival(k, 0)
            even_arrival(k, 1)
            return carry

        lax.fori_loop(low, high, take, 0)

    def t_copy(d):
        return remote(
            t_send.at[d + REACH], t_recv.at[REACH - d], t_s.at[d + REACH], t_r.at[REACH - d], row_peer(d)
        )

    def t_arrival(d):
        return remote(t_send.at[d + REACH], t_recv.at[d + REACH], t_s.at[d + REACH], t_r.at[d + REACH], row_peer(d))

    def vertical(window_ref, store):
        window = jnp.concatenate([kept(window_ref[d + REACH], band + d, bands) for d in diagonals], axis=0)
        for r in range(rank_count):
            store[r] = dot(vert[r], window, ((1,), (0,))).astype(BF16)

    def part_copy(i):
        owner = 2 * odd_chip(i) + 1
        k = skew + 2 * i
        return remote(part_send.at[i], part_recv.at[k], part_s.at[i], part_r.at[k], (owner, band))

    own_share = (core == 1) & (skew == 0)

    for position, i in enumerate(order_b):
        for d in steps:
            tb_arrival(i, d).wait_recv()
        vertical(tb_recv.at[i], part_send.at[i])
        if i == 0:

            @pl.when(own_share)
            def _():
                part_recv[0] = part_send[0]

            @pl.when(jnp.logical_not(own_share))
            def _():
                part_copy(0).start()

        else:
            part_copy(i).start()

        @pl.when(core == 0)
        def _():
            if position == 0:
                own_even.wait()
                add_frames(me, True)
                even_arrival(0, 1)
                gather_even(1, 3)
            if position == 1:
                gather_even(3, 5)
            if position == 2:
                gather_even(5, chips)
                for d in steps:
                    t_send[d + REACH] = sums[d + REACH].astype(BF16)
                    t_copy(d).start()
                t_recv[REACH] = sums[REACH].astype(BF16)

    @pl.when(core == 0)
    def _():
        for d in steps:
            t_arrival(d).wait_recv()
        vertical(t_recv, rowed_ref)

    def part_arrival(k):
        remote(part_send.at[0], part_recv.at[k], part_s.at[0], part_r.at[k], (sibling, band)).wait_recv()

    @pl.when(core == 1)
    def _():
        @pl.when(jnp.logical_not(own_share))
        def _():
            part_arrival(0)

        for k in range(1, chips):
            part_arrival(k)
        for r in range(rank_count):
            total = part_recv[0, r].astype(F32)
            for k in range(1, chips):
                total = total + part_recv[k, r].astype(F32)
            rowed_ref[r] = total.astype(BF16)

    def p_copy(d):
        return remote(
            p_send.at[d + REACH], p_recv.at[d + REACH], p_s.at[d + REACH], p_r.at[d + REACH], frame_peer(-d)
        )

    rowed = [rowed_ref[r] for r in range(rank_count)]
    measured = None
    for d in steps + [0]:
        total = None
        for r in range(rank_count):
            term = dot(rowed[r], horiz[r, :, (d + REACH) * block : (d + REACH + 1) * block], ((1,), (1,)))
            total = term if total is None else total + term
        if d == 0:
            measured = total
        else:
            p_send[d + REACH] = total.astype(BF16)
            p_copy(d).start()
    for d in steps:
        p_copy(d).wait_recv()
        measured = measured + kept(p_recv[d + REACH].astype(F32), me + d, frame_devices)
    sensor_copy.wait()
    res_recv[REACH] = (measured - sensor_buf[...]).astype(BF16)

    def r_copy(d):
        return remote(
            res_recv.at[REACH], res_recv.at[d + REACH], r_s.at[d + REACH], r_r.at[d + REACH], frame_peer(d)
        )

    for d in steps:
        r_copy(d).start()
    for d in steps:
        r_copy(d).wait_recv()
    pieces = [kept(res_recv[d + REACH], me - d, frame_devices) for d in diagonals]
    for r in range(rank_count):
        total = None
        for d in diagonals:
            term = dot(pieces[d + REACH], horiz[r, :, (d + REACH) * block : (d + REACH + 1) * block], ((1,), (0,)))
            total = term if total is None else total + term
        spread[r] = total.astype(BF16)

    def q_copy(k):
        target = 2 * wrap(chip - k, chips) + lax.rem(chip, 2)
        return remote(spread, q_recv.at[k // 2], q_s.at[k], q_r.at[k // 2], (target, band))

    @pl.when(core == 1)
    def _():
        for k in [4, 5, 3, 6, 2, 7, 1]:
            q_copy(k).start()

        @pl.when(own_share)
        def _():
            q_recv[0] = spread[...]

        @pl.when(jnp.logical_not(own_share))
        def _():
            q_copy(0).start()

    def adjoint(tile_ref, store, keep):
        lhs = vert[...].reshape(rank_count * block, DIAGS * block)
        rhs = tile_ref[...].reshape(rank_count * block, slice_cols)
        products = dot(lhs, rhs, ((0,), (0,))).astype(BF16)
        for d in diagonals:
            target = keep if d == 0 else store
            target[d + REACH] = products[(d + REACH) * block : (d + REACH + 1) * block]

    def h_copy(d):
        return remote(
            h_send.at[d + REACH], h_recv.at[d + REACH], h_s.at[d + REACH], h_r.at[d + REACH], row_peer(d)
        )

    @pl.when(core == 0)
    def _():
        adjoint(spread, h_send, h_recv)
        for d in steps:
            h_copy(d).start()

    def hb_copy(i, d):
        return remote(
            hb_send.at[i, d + REACH], hb_recv.at[i, d + REACH], hb_s.at[i, d + REACH], hb_r.at[i, d + REACH], row_peer(d)
        )

    def gradient(sources_ref, frame, part):
        return weighted(
            [(sources_ref[d + REACH, part].astype(F32), on(frame, band - d)) for d in diagonals]
        ).astype(BF16)

    def g_copy(k):
        target = wrap(me + k, frame_devices)
        distance = wrap(target // 2 - chip, chips)
        return remote(
            g_send.at[target], grad_ref.at[:, :, columns(me)], g_s.at[k], g_r.at[distance], (target, band)
        )

    def give(q, carry):
        k = chips + ((q + 1) // 2) * (2 * lax.rem(q, 2) - 1)
        target = wrap(me + k, frame_devices)
        for f in range(local_count):
            g_send[target, f] = gradient(h_recv, target * local_count + f, slice(None))
        g_copy(k).start()
        return carry

    def q_arrival(i):
        remote(spread, q_recv.at[i], q_s.at[0], q_r.at[i], (sibling, band)).wait_recv()

    for position, i in enumerate([0, 3, 1, 2]):
        if i == 0:

            @pl.when(jnp.logical_not(own_share))
            def _():
                q_arrival(0)

        else:
            q_arrival(i)
        adjoint(q_recv.at[i], hb_send.at[i], hb_recv.at[i])
        for d in steps:
            hb_copy(i, d).start()
        if position == 1:

            @pl.when(core == 0)
            def _():
                for d in steps:
                    h_copy(d).wait_recv()
                lax.fori_loop(0, frame_devices - 1, give, 0)
                for f in range(local_count):
                    grad_ref[f, :, columns(me)] = gradient(h_recv, me * local_count + f, slice(None))

    def gb_copy(i):
        return remote(
            gb_send.at[i], grad_ref.at[:, :, columns(2 * odd_chip(i) + 1)], gb_s.at[i], gb_r.at[i], (sibling, band)
        )

    def gb_arrival(i):
        index = 2 * lax.rem(chip + 1 - skew + 2 * i, chips) + 1
        return remote(gb_send.at[i], grad_ref.at[:, :, columns(index)], gb_s.at[i], gb_r.at[i], (sibling, band))

    for i in [0, 3, 1, 2]:
        for d in steps:
            hb_copy(i, d).wait_recv()
        for f in range(local_count):
            gb_send[i, f] = gradient(hb_recv.at[i], sibling * local_count + f, slice(None))
        gb_copy(i).start()
        for f in range(local_count):
            grad_ref[f, :, columns(2 * odd_chip(i) + 1)] = gradient(
                hb_recv.at[i], me * local_count + f, slice(None)
            )

    def g_arrival(k):
        index = 2 * wrap(chip - k, chips)
        remote(g_send.at[0], grad_ref.at[:, :, columns(index)], g_s.at[0], g_r.at[k], (sibling, band)).wait_recv()

    for k in range(1, chips):
        g_arrival(k)

    @pl.when(core == 1)
    def _():
        g_arrival(0)
        even_copy(0).wait_send()
        for k in range(1, chips):
            q_copy(k).wait_send()

        @pl.when(jnp.logical_not(own_share))
        def _():
            q_copy(0).wait_send()

    @pl.when(core == 0)
    def _():
        def depart(k, carry):
            g_copy(k).wait_send()
            return carry

        lax.fori_loop(1, frame_devices, depart, 0)
        for d in steps:
            t_copy(d).wait_send()
            h_copy(d).wait_send()

    @pl.when(jnp.logical_not(own_share))
    def _():
        part_copy(0).wait_send()

    for k in range(1, chips):
        even_copy(k).wait_send()
    for i in range(shares):
        gb_arrival(i).wait_recv()
        gb_copy(i).wait_send()
        swap_copy(i).wait_send()
        if i > 0:
            part_copy(i).wait_send()
        for d in steps:
            tb_copy(i, d).wait_send()
            hb_copy(i, d).wait_send()
    for d in steps:
        p_copy(d).wait_send()
        r_copy(d).wait_send()


def per_device(
    video_frames, split_frames, dual_frames, sensor_image, kernel_vertical, kernel_horizontal, shutter_start, shutter_end
):
    local_count, block, width = video_frames.shape
    rank_count, taps = kernel_vertical.shape
    frame_devices = lax.axis_size("frame")
    slice_cols = width // frame_devices
    chips = frame_devices // 2
    shares = chips // 2
    hbm = pl.BlockSpec(memory_space=pltpu.HBM)
    dma = pltpu.SemaphoreType.DMA
    tile = (block, slice_cols)
    operands = (shutter_start, shutter_end, video_frames, sensor_image, kernel_vertical, kernel_horizontal)
    gradient = pl.pallas_call(
        kernel,
        out_shape=jax.ShapeDtypeStruct((local_count, block, width), BF16),
        in_specs=[hbm] * 6,
        out_specs=pl.BlockSpec(memory_space=pltpu.VMEM),
        scratch_shapes=[
            pltpu.SMEM(shutter_start.shape, jnp.int32),
            pltpu.SMEM(shutter_end.shape, jnp.int32),
            pltpu.VMEM((rank_count, taps), BF16),
            pltpu.VMEM((rank_count, taps), BF16),
            pltpu.VMEM(tile, F32),
            pltpu.VMEM((rank_count, block, taps + block), BF16),
            pltpu.VMEM((rank_count, block, taps + block), BF16),
            pltpu.VMEM((DIAGS,) + tile, F32),
        ]
        + [
            pltpu.VMEM(lead + tile, BF16)
            for lead in [
                (rank_count,), (rank_count,),
                (frame_devices, local_count), (shares, local_count), (shares, local_count),
                (shares, DIAGS), (shares, DIAGS), (shares, rank_count), (chips, rank_count),
                (DIAGS,), (DIAGS,), (DIAGS,), (DIAGS,), (DIAGS,), (DIAGS,), (DIAGS,),
                (shares, rank_count), (shares, DIAGS), (shares, DIAGS),
                (frame_devices, local_count), (shares, local_count),
            ]
        ]
        + [
            dma(count)
            for count in [
                (6,), (shares,), (shares,), (shares,), (chips,), (frame_devices,),
                (shares, DIAGS), (shares, DIAGS), (shares,), (chips,), (DIAGS,), (DIAGS,),
                (DIAGS,), (DIAGS,), (DIAGS,), (DIAGS,), (DIAGS,), (DIAGS,), (chips,), (shares,),
                (shares, DIAGS), (shares, DIAGS), (frame_devices,), (chips,), (shares,), (shares,),
            ]
        ],
        compiler_params=pltpu.CompilerParams(
            collective_id=0, has_side_effects=True, vmem_limit_bytes=32 << 20
        ),
        name="blur_and_adjoint",
    )(*[pltpu.with_memory_space_constraint(x, pltpu.HBM) for x in operands])
    current = video_frames.astype(F32)
    dual_value = dual_frames.astype(F32)
    moved_frames = current - tau_step * (
        gradient.astype(F32) + rho_weight * (current - split_frames.astype(F32) + dual_value)
    )
    shifted = moved_frames + dual_value
    clamped = jnp.maximum(shifted, 0.0)
    return (
        moved_frames.astype(BF16),
        clamped.astype(BF16),
        (shifted - clamped).astype(BF16),
    )


def solution(mesh):
    frames = P("frame", "row", None)
    return jax.shard_map(
        per_device,
        mesh=mesh,
        in_specs=(frames, frames, frames, P("row", None), P(), P(), P(), P()),
        out_specs=(frames, frames, frames),
        check_vma=False,
    )
```

```python
import functools

import jax
import jax.numpy as jnp
from jax import lax
from jax.experimental import pallas as pl
from jax.experimental.pallas import tpu as pltpu
from jax.sharding import PartitionSpec as P

MESH = pl.DeviceIdType.MESH
tau_step = 0.1
rho_weight = 2.0
REACH = 3
DIAGS = 2 * REACH + 1
F32 = jnp.float32
BF16 = jnp.bfloat16


def dot(a, b, contract):
    return lax.dot_general(a, b, (contract, ((), ())), preferred_element_type=F32)


def far_first(count):
    return sorted(range(1, count), key=lambda k: -min(k, count - k))


def wrap(index, count):
    return lax.rem(index + count, count)


def banded(kernel_ref, scratch, block):
    rank_count, taps = kernel_ref.shape
    padded = jnp.concatenate(
        [kernel_ref[...].astype(F32), jnp.zeros((rank_count, block), F32)], axis=1
    )
    for r in range(rank_count):
        rows = jnp.broadcast_to(padded[r : r + 1], (block, taps + block))
        scratch[r] = pltpu.roll(rows, 0, 1, stride=1, stride_axis=0)


def spans(count, block):
    return [slice(i * block, (i + 1) * block) for i in range(count)]


def kernel(
    start_hbm, end_hbm, video_ref, sensor_ref, kv_hbm, kh_hbm, split_ref, dual_ref, grad_ref, base_ref,
    video_buf, split_buf, dual_buf,
    start_ref, end_ref, kv_ref, kh_ref, sensor_buf, bands_f32, vert, vert_t, horiz_p, horiz_q, sums, rowed_ref, spread,
    frames_buf, own_buf, swap_buf, tb_send, tb_recv, part_send, part_recv, t_send, t_recv,
    p_send, p_recv, res_recv, h_send, h_recv, q_recv, hb_send, hb_recv, g_send, gb_send,
    local_sem, own_sem, sw_s, sw_r, a_s, a_r, tb_s, tb_r, part_s, part_r, t_s, t_r,
    p_s, p_r, r_s, r_r, h_s, h_r, q_s, q_r, hb_s, hb_r, g_s, g_r, gb_s, gb_r,
):
    frame_devices, local_count, block, slice_cols = frames_buf.shape
    chips = frame_devices // 2
    shares = chips // 2
    bands = start_ref.shape[0]
    rank_count = kv_ref.shape[0]
    me = lax.axis_index("frame")
    band = lax.axis_index("row")
    chip = me // 2
    core = lax.rem(me, 2)
    sibling = me + 1 - 2 * core
    skew = lax.rem(core + chip, 2)
    steps = [3, -3, 2, -2, 1, -1]
    diagonals = range(-REACH, REACH + 1)

    def frame_peer(d):
        return (wrap(me + d, frame_devices), band)

    def row_peer(d):
        return (me, wrap(band + d, bands))

    def columns(index):
        return pl.ds(pl.multiple_of(index * slice_cols, slice_cols), slice_cols)

    def odd_chip(i):
        return lax.rem(chip + skew + 2 * i, chips)

    def remote(src, dst, send_sem, recv_sem, target):
        return pltpu.make_async_remote_copy(
            src_ref=src, dst_ref=dst, send_sem=send_sem, recv_sem=recv_sem,
            device_id=target, device_id_type=MESH,
        )

    small = [
        pltpu.make_async_copy(src, dst, local_sem.at[2 + i])
        for i, (src, dst) in enumerate(
            [(start_hbm, start_ref), (end_hbm, end_ref), (kv_hbm, kv_ref), (kh_hbm, kh_ref)]
        )
    ]
    for copy in small:
        copy.start()
    own_copies = [
        pltpu.make_async_copy(video_ref.at[:, :, columns(2 * odd_chip(i) + 1)], own_buf.at[i], own_sem.at[i])
        for i in range(shares)
    ]
    for copy in own_copies:
        copy.start()
    own_even = pltpu.make_async_copy(video_ref.at[:, :, columns(2 * chip)], frames_buf.at[me], local_sem.at[0])
    sensor_copy = pltpu.make_async_copy(sensor_ref.at[:, columns(me)], sensor_buf, local_sem.at[1])
    sensor_copy.start()

    @pl.when(core == 0)
    def _():
        own_even.start()

    barrier = pltpu.get_barrier_semaphore()

    def greet(k, carry):
        pl.semaphore_signal(barrier, inc=1, device_id=frame_peer(k), device_id_type=MESH)
        return carry

    for k in far_first(frame_devices):
        greet(k, 0)
    for d in steps:
        pl.semaphore_signal(barrier, inc=1, device_id=row_peer(d), device_id_type=MESH)
    pl.semaphore_wait(barrier, frame_devices - 1 + len(steps))

    def swap_copy(i):
        index = 2 * lax.rem(chip + 1 - skew + 2 * i, chips) + 1
        return remote(video_ref.at[:, :, columns(index)], swap_buf.at[i], sw_s.at[i], sw_r.at[i], (sibling, band))

    def even_copy(k):
        target = 2 * lax.rem(chip + k, chips)
        return remote(
            video_ref.at[:, :, columns(target)], frames_buf.at[me], a_s.at[k], a_r.at[2 * k + core], (target, band)
        )

    order_b = [2, 1, 3, 0]
    for i in order_b:
        swap_copy(i).start()

    for k in far_first(chips):
        even_copy(k).start()

    @pl.when(core == 1)
    def _():
        even_copy(0).start()

    loads = [
        pltpu.make_async_copy(src, dst, local_sem.at[6 + i])
        for i, (src, dst) in enumerate([(video_ref, video_buf), (split_ref, split_buf), (dual_ref, dual_buf)])
    ]
    for copy in loads:
        copy.start()
    for copy in small[:2]:
        copy.wait()

    def on(frame, band_index):
        inside = (band_index >= 0) & (band_index < bands)
        at = jnp.clip(band_index, 0, bands - 1)
        active = inside & (start_ref[at] <= frame) & (frame < end_ref[at])
        return jnp.where(active, 1.0, 0.0).astype(F32)

    def kept(value, index, count):
        return value * jnp.where((index >= 0) & (index < count), 1.0, 0.0).astype(value.dtype)

    def weighted(pairs):
        total = None
        for value, weight in pairs:
            total = value * weight if total is None else total + value * weight
        return total

    def tb_copy(i, d):
        return remote(
            tb_send.at[i, d + REACH], tb_recv.at[i, REACH - d], tb_s.at[i, d + REACH], tb_r.at[i, REACH - d], row_peer(d)
        )

    def tb_arrival(i, d):
        return remote(tb_send.at[i, d + REACH], tb_recv.at[i, d + REACH], tb_s.at[i, d + REACH], tb_r.at[i, d + REACH], row_peer(d))

    half = block // 4
    for i in order_b:
        own_copies[i].wait()
        swap_copy(i).wait_recv()

        def mix(c, carry):
            part = pl.ds(pl.multiple_of(c * half, half), half)
            mine = [(own_buf[i, f, part].astype(F32), me * local_count + f) for f in range(local_count)]
            others = [(swap_buf[i, f, part].astype(F32), sibling * local_count + f) for f in range(local_count)]
            for d in diagonals:
                total = weighted([(value, on(frame, band + d)) for value, frame in mine + others]).astype(BF16)
                if d == 0:
                    tb_recv[i, REACH, part] = total
                else:
                    tb_send[i, d + REACH, part] = total
            return carry

        lax.fori_loop(0, 4, mix, 0)
        for d in steps:
            tb_copy(i, d).start()

    for copy in small[2:]:
        copy.wait()
    ranks = spans(rank_count, block)
    blocks = spans(DIAGS, block)
    banded(kv_ref, bands_f32, block)
    for r in range(rank_count):
        vert[ranks[r]] = bands_f32[r].astype(BF16)
        for cols in blocks:
            vert_t[cols, ranks[r]] = bands_f32[r, :, cols].T.astype(BF16)
    banded(kh_ref, bands_f32, block)
    for r in range(rank_count):
        for cols in blocks:
            horiz_p[ranks[r], cols] = bands_f32[r, :, cols].T.astype(BF16)
            horiz_q[cols, ranks[r]] = bands_f32[r, :, cols].astype(BF16)

    for copy in loads:
        copy.wait()

    def pull(c, carry):
        part = pl.ds(pl.multiple_of(c * 16, 16), 16)
        for f in range(local_count):
            current = video_buf[f, part].astype(F32)
            apart = current - split_buf[f, part].astype(F32) + dual_buf[f, part].astype(F32)
            base_ref[f, part] = current - tau_step * rho_weight * apart
        return carry

    lax.fori_loop(0, block // 16, pull, 0)

    def add_frames(source, first):
        for d in diagonals:
            total = None if first else sums[d + REACH]
            for f in range(local_count):
                term = frames_buf[source, f].astype(F32) * on(source * local_count + f, band + d)
                total = term if total is None else total + term
            sums[d + REACH] = total

    def even_arrival(k, from_core):
        source = 2 * wrap(chip - k, chips) + from_core
        remote(frames_buf.at[source], frames_buf.at[source], a_s.at[k], a_r.at[2 * k + from_core], (sibling, band)).wait_recv()
        add_frames(source, False)

    def gather_even(low, high):
        def take(q, carry):
            k = wrap(((q + 1) // 2) * (2 * lax.rem(q, 2) - 1), chips)
            even_arrival(k, 0)
            even_arrival(k, 1)
            return carry

        lax.fori_loop(low, high, take, 0)

    def t_copy(d):
        return remote(
            t_send.at[d + REACH], t_recv.at[REACH - d], t_s.at[d + REACH], t_r.at[REACH - d], row_peer(d)
        )

    def t_arrival(d):
        return remote(t_send.at[d + REACH], t_recv.at[d + REACH], t_s.at[d + REACH], t_r.at[d + REACH], row_peer(d))

    def vertical(window_ref, store):
        window = jnp.concatenate([kept(window_ref[d + REACH], band + d, bands) for d in diagonals], axis=0)
        products = dot(vert[...], window, ((1,), (0,))).astype(BF16)
        for r in range(rank_count):
            store[r] = products[ranks[r]]

    def part_copy(i):
        owner = 2 * odd_chip(i) + 1
        k = skew + 2 * i
        return remote(part_send.at[i], part_recv.at[k], part_s.at[i], part_r.at[k], (owner, band))

    own_share = (core == 1) & (skew == 0)

    for position, i in enumerate(order_b):
        for d in steps:
            tb_arrival(i, d).wait_recv()
        vertical(tb_recv.at[i], part_send.at[i])
        if i == 0:

            @pl.when(own_share)
            def _():
                part_recv[0] = part_send[0]

            @pl.when(jnp.logical_not(own_share))
            def _():
                part_copy(0).start()

        else:
            part_copy(i).start()

        @pl.when(core == 0)
        def _():
            if position == 0:
                own_even.wait()
                add_frames(me, True)
                even_arrival(0, 1)
                gather_even(1, 3)
            if position == 1:
                gather_even(3, 5)
            if position == 2:
                gather_even(5, chips)
                for d in steps:
                    t_send[d + REACH] = sums[d + REACH].astype(BF16)
                    t_copy(d).start()
                t_recv[REACH] = sums[REACH].astype(BF16)

    @pl.when(core == 0)
    def _():
        for d in steps:
            t_arrival(d).wait_recv()
        vertical(t_recv, rowed_ref)

    def part_arrival(k):
        remote(part_send.at[0], part_recv.at[k], part_s.at[0], part_r.at[k], (sibling, band)).wait_recv()

    @pl.when(core == 1)
    def _():
        @pl.when(jnp.logical_not(own_share))
        def _():
            part_arrival(0)

        for k in range(1, chips):
            part_arrival(k)
        for r in range(rank_count):
            total = part_recv[0, r].astype(F32)
            for k in range(1, chips):
                total = total + part_recv[k, r].astype(F32)
            rowed_ref[r] = total.astype(BF16)

    def p_copy(d):
        return remote(
            p_send.at[d + REACH], p_recv.at[d + REACH], p_s.at[d + REACH], p_r.at[d + REACH], frame_peer(-d)
        )

    rowed = jnp.concatenate([rowed_ref[r] for r in range(rank_count)], axis=1)
    products = dot(rowed, horiz_p[...], ((1,), (0,)))
    for d in steps:
        p_send[d + REACH] = products[:, blocks[d + REACH]].astype(BF16)
        p_copy(d).start()
    measured = products[:, blocks[REACH]]
    for d in steps:
        p_copy(d).wait_recv()
        measured = measured + kept(p_recv[d + REACH].astype(F32), me + d, frame_devices)
    sensor_copy.wait()
    res_recv[REACH] = (measured - sensor_buf[...]).astype(BF16)

    def r_copy(d):
        return remote(
            res_recv.at[REACH], res_recv.at[d + REACH], r_s.at[d + REACH], r_r.at[d + REACH], frame_peer(d)
        )

    for d in steps:
        r_copy(d).start()
    for d in steps:
        r_copy(d).wait_recv()
    pieces = jnp.concatenate([kept(res_recv[d + REACH], me - d, frame_devices) for d in diagonals], axis=1)
    products = dot(pieces, horiz_q[...], ((1,), (0,))).astype(BF16)
    for r in range(rank_count):
        spread[r] = products[:, ranks[r]]

    def q_copy(k):
        target = 2 * wrap(chip - k, chips) + lax.rem(chip, 2)
        return remote(spread, q_recv.at[k // 2], q_s.at[k], q_r.at[k // 2], (target, band))

    @pl.when(core == 1)
    def _():
        for k in [4, 5, 3, 6, 2, 7, 1]:
            q_copy(k).start()

        @pl.when(own_share)
        def _():
            q_recv[0] = spread[...]

        @pl.when(jnp.logical_not(own_share))
        def _():
            q_copy(0).start()

    def adjoint(tile_ref, store, keep):
        tile = tile_ref[...].reshape(rank_count * block, slice_cols)
        products = dot(vert_t[...], tile, ((1,), (0,))).astype(BF16)
        for d in diagonals:
            target = keep if d == 0 else store
            target[d + REACH] = products[blocks[d + REACH]]

    def h_copy(d):
        return remote(
            h_send.at[d + REACH], h_recv.at[d + REACH], h_s.at[d + REACH], h_r.at[d + REACH], row_peer(d)
        )

    @pl.when(core == 0)
    def _():
        adjoint(spread, h_send, h_recv)
        for d in steps:
            h_copy(d).start()

    def hb_copy(i, d):
        return remote(
            hb_send.at[i, d + REACH], hb_recv.at[i, d + REACH], hb_s.at[i, d + REACH], hb_r.at[i, d + REACH], row_peer(d)
        )

    def gradient(sources_ref, frame, part):
        return weighted(
            [(sources_ref[d + REACH, part].astype(F32), on(frame, band - d)) for d in diagonals]
        ).astype(BF16)

    def g_copy(k):
        target = wrap(me + k, frame_devices)
        distance = wrap(target // 2 - chip, chips)
        return remote(
            g_send.at[target], grad_ref.at[:, :, columns(me)], g_s.at[k], g_r.at[distance], (target, band)
        )

    def give(q, carry):
        k = chips + ((q + 1) // 2) * (2 * lax.rem(q, 2) - 1)
        target = wrap(me + k, frame_devices)
        for f in range(local_count):
            g_send[target, f] = gradient(h_recv, target * local_count + f, slice(None))
        g_copy(k).start()
        return carry

    def q_arrival(i):
        remote(spread, q_recv.at[i], q_s.at[0], q_r.at[i], (sibling, band)).wait_recv()

    for position, i in enumerate([0, 3, 1, 2]):
        if i == 0:

            @pl.when(jnp.logical_not(own_share))
            def _():
                q_arrival(0)

        else:
            q_arrival(i)
        adjoint(q_recv.at[i], hb_send.at[i], hb_recv.at[i])
        for d in steps:
            hb_copy(i, d).start()
        if position == 0:

            @pl.when(core == 0)
            def _():
                for d in steps:
                    h_copy(d).wait_recv()
                lax.fori_loop(0, frame_devices - 1, give, 0)
                for f in range(local_count):
                    grad_ref[f, :, columns(me)] = gradient(h_recv, me * local_count + f, slice(None))

    def gb_copy(i):
        return remote(
            gb_send.at[i], grad_ref.at[:, :, columns(2 * odd_chip(i) + 1)], gb_s.at[i], gb_r.at[i], (sibling, band)
        )

    def gb_arrival(i):
        index = 2 * lax.rem(chip + 1 - skew + 2 * i, chips) + 1
        return remote(gb_send.at[i], grad_ref.at[:, :, columns(index)], gb_s.at[i], gb_r.at[i], (sibling, band))

    for i in [0, 3, 1, 2]:
        for d in steps:
            hb_copy(i, d).wait_recv()
        for f in range(local_count):
            gb_send[i, f] = gradient(hb_recv.at[i], sibling * local_count + f, slice(None))
        gb_copy(i).start()
        for f in range(local_count):
            grad_ref[f, :, columns(2 * odd_chip(i) + 1)] = gradient(
                hb_recv.at[i], me * local_count + f, slice(None)
            )

    def g_arrival(k):
        index = 2 * wrap(chip - k, chips)
        remote(g_send.at[0], grad_ref.at[:, :, columns(index)], g_s.at[0], g_r.at[k], (sibling, band)).wait_recv()

    for k in range(1, chips):
        g_arrival(k)

    @pl.when(core == 1)
    def _():
        g_arrival(0)
        even_copy(0).wait_send()
        for k in range(1, chips):
            q_copy(k).wait_send()

        @pl.when(jnp.logical_not(own_share))
        def _():
            q_copy(0).wait_send()

    @pl.when(core == 0)
    def _():
        def depart(k, carry):
            g_copy(k).wait_send()
            return carry

        lax.fori_loop(1, frame_devices, depart, 0)
        for d in steps:
            t_copy(d).wait_send()
            h_copy(d).wait_send()

    @pl.when(jnp.logical_not(own_share))
    def _():
        part_copy(0).wait_send()

    for k in range(1, chips):
        even_copy(k).wait_send()
    for i in range(shares):
        gb_arrival(i).wait_recv()
        gb_copy(i).wait_send()
        swap_copy(i).wait_send()
        if i > 0:
            part_copy(i).wait_send()
        for d in steps:
            tb_copy(i, d).wait_send()
            hb_copy(i, d).wait_send()
    for d in steps:
        p_copy(d).wait_send()
        r_copy(d).wait_send()


def per_device(
    video_frames, split_frames, dual_frames, sensor_image, kernel_vertical, kernel_horizontal, shutter_start, shutter_end
):
    local_count, block, width = video_frames.shape
    rank_count, taps = kernel_vertical.shape
    frame_devices = lax.axis_size("frame")
    slice_cols = width // frame_devices
    chips = frame_devices // 2
    shares = chips // 2
    hbm = pl.BlockSpec(memory_space=pltpu.HBM)
    dma = pltpu.SemaphoreType.DMA
    tile = (block, slice_cols)
    operands = (shutter_start, shutter_end, video_frames, sensor_image, kernel_vertical, kernel_horizontal, split_frames, dual_frames)
    gradient, base = pl.pallas_call(
        kernel,
        out_shape=[jax.ShapeDtypeStruct((local_count, block, width), kind) for kind in (BF16, F32)],
        in_specs=[hbm] * 8,
        out_specs=[pl.BlockSpec(memory_space=pltpu.VMEM)] * 2,
        scratch_shapes=[pltpu.VMEM((local_count, block, width), BF16)] * 3
        + [
            pltpu.SMEM(shutter_start.shape, jnp.int32),
            pltpu.SMEM(shutter_end.shape, jnp.int32),
            pltpu.VMEM((rank_count, taps), BF16),
            pltpu.VMEM((rank_count, taps), BF16),
            pltpu.VMEM(tile, F32),
            pltpu.VMEM((rank_count, block, taps + block), F32),
            pltpu.VMEM((rank_count * block, taps + block), BF16),
            pltpu.VMEM((taps + block, rank_count * block), BF16),
            pltpu.VMEM((rank_count * block, taps + block), BF16),
            pltpu.VMEM((taps + block, rank_count * block), BF16),
            pltpu.VMEM((DIAGS,) + tile, F32),
        ]
        + [
            pltpu.VMEM(lead + tile, BF16)
            for lead in [
                (rank_count,), (rank_count,),
                (frame_devices, local_count), (shares, local_count), (shares, local_count),
                (shares, DIAGS), (shares, DIAGS), (shares, rank_count), (chips, rank_count),
                (DIAGS,), (DIAGS,), (DIAGS,), (DIAGS,), (DIAGS,), (DIAGS,), (DIAGS,),
                (shares, rank_count), (shares, DIAGS), (shares, DIAGS),
                (frame_devices, local_count), (shares, local_count),
            ]
        ]
        + [
            dma(count)
            for count in [
                (9,), (shares,), (shares,), (shares,), (chips,), (frame_devices,),
                (shares, DIAGS), (shares, DIAGS), (shares,), (chips,), (DIAGS,), (DIAGS,),
                (DIAGS,), (DIAGS,), (DIAGS,), (DIAGS,), (DIAGS,), (DIAGS,), (chips,), (shares,),
                (shares, DIAGS), (shares, DIAGS), (frame_devices,), (chips,), (shares,), (shares,),
            ]
        ],
        compiler_params=pltpu.CompilerParams(
            collective_id=0, has_side_effects=True, vmem_limit_bytes=32 << 20
        ),
        name="blur_and_adjoint",
    )(*[pltpu.with_memory_space_constraint(x, pltpu.HBM) for x in operands])
    moved_frames = base - tau_step * gradient.astype(F32)
    shifted = moved_frames + dual_frames.astype(F32)
    clamped = jnp.maximum(shifted, 0.0)
    return (
        moved_frames.astype(BF16),
        clamped.astype(BF16),
        (shifted - clamped).astype(BF16),
    )


def solution(mesh):
    frames = P("frame", "row", None)
    return jax.shard_map(
        per_device,
        mesh=mesh,
        in_specs=(frames, frames, frames, P("row", None), P(), P(), P(), P()),
        out_specs=(frames, frames, frames),
        check_vma=False,
    )
```

```python
import functools

import jax
import jax.numpy as jnp
from jax import lax
from jax.experimental import pallas as pl
from jax.experimental.pallas import tpu as pltpu
from jax.sharding import PartitionSpec as P

MESH = pl.DeviceIdType.MESH
tau_step = 0.1
rho_weight = 2.0
REACH = 3
DIAGS = 2 * REACH + 1
F32 = jnp.float32
BF16 = jnp.bfloat16


def dot(a, b, contract):
    return lax.dot_general(a, b, (contract, ((), ())), preferred_element_type=F32)


def far_first(count):
    return sorted(range(1, count), key=lambda k: -min(k, count - k))


def wrap(index, count):
    return lax.rem(index + count, count)


def banded(kernel_ref, scratch, block):
    rank_count, taps = kernel_ref.shape
    padded = jnp.concatenate(
        [kernel_ref[...].astype(F32), jnp.zeros((rank_count, block), F32)], axis=1
    )
    for r in range(rank_count):
        rows = jnp.broadcast_to(padded[r : r + 1], (block, taps + block))
        scratch[r] = pltpu.roll(rows, 0, 1, stride=1, stride_axis=0)


def spans(count, block):
    return [slice(i * block, (i + 1) * block) for i in range(count)]


def kernel(
    start_hbm, end_hbm, video_ref, sensor_ref, kv_hbm, kh_hbm, split_ref, dual_ref, grad_ref, base_ref,
    video_buf, split_buf, dual_buf,
    start_ref, end_ref, kv_ref, kh_ref, sensor_buf, bands_f32, vert, vert_t, horiz_p, horiz_q, sums, rowed_ref, spread,
    frames_buf, own_buf, swap_buf, tb_send, tb_recv, part_send, part_recv, t_send, t_recv,
    p_send, p_recv, res_recv, h_send, h_recv, q_recv, hb_send, hb_recv, g_send, gb_send,
    local_sem, own_sem, sw_s, sw_r, a_s, a_r, tb_s, tb_r, part_s, part_r, t_s, t_r,
    p_s, p_r, r_s, r_r, h_s, h_r, q_s, q_r, hb_s, hb_r, g_s, g_r, gb_s, gb_r,
):
    frame_devices, local_count, block, slice_cols = frames_buf.shape
    chips = frame_devices // 2
    shares = chips // 2
    bands = start_ref.shape[0]
    rank_count = kv_ref.shape[0]
    me = lax.axis_index("frame")
    band = lax.axis_index("row")
    chip = me // 2
    core = lax.rem(me, 2)
    sibling = me + 1 - 2 * core
    skew = lax.rem(core + chip, 2)
    steps = [3, -3, 2, -2, 1, -1]
    diagonals = range(-REACH, REACH + 1)

    def frame_peer(d):
        return (wrap(me + d, frame_devices), band)

    def row_peer(d):
        return (me, wrap(band + d, bands))

    def columns(index):
        return pl.ds(pl.multiple_of(index * slice_cols, slice_cols), slice_cols)

    def odd_chip(i):
        return lax.rem(chip + skew + 2 * i, chips)

    def remote(src, dst, send_sem, recv_sem, target):
        return pltpu.make_async_remote_copy(
            src_ref=src, dst_ref=dst, send_sem=send_sem, recv_sem=recv_sem,
            device_id=target, device_id_type=MESH,
        )

    small = [
        pltpu.make_async_copy(src, dst, local_sem.at[2 + i])
        for i, (src, dst) in enumerate(
            [(start_hbm, start_ref), (end_hbm, end_ref), (kv_hbm, kv_ref), (kh_hbm, kh_ref)]
        )
    ]
    for copy in small:
        copy.start()
    own_copies = [
        pltpu.make_async_copy(video_ref.at[:, :, columns(2 * odd_chip(i) + 1)], own_buf.at[i], own_sem.at[i])
        for i in range(shares)
    ]
    for copy in own_copies:
        copy.start()
    own_even = pltpu.make_async_copy(video_ref.at[:, :, columns(2 * chip)], frames_buf.at[me], local_sem.at[0])
    sensor_copy = pltpu.make_async_copy(sensor_ref.at[:, columns(me)], sensor_buf, local_sem.at[1])
    sensor_copy.start()

    @pl.when(core == 0)
    def _():
        own_even.start()

    barrier = pltpu.get_barrier_semaphore()

    def greet(k, carry):
        pl.semaphore_signal(barrier, inc=1, device_id=frame_peer(k), device_id_type=MESH)
        return carry

    for k in far_first(frame_devices):
        greet(k, 0)
    for d in steps:
        pl.semaphore_signal(barrier, inc=1, device_id=row_peer(d), device_id_type=MESH)
    pl.semaphore_wait(barrier, frame_devices - 1 + len(steps))

    def swap_copy(i):
        index = 2 * lax.rem(chip + 1 - skew + 2 * i, chips) + 1
        return remote(video_ref.at[:, :, columns(index)], swap_buf.at[i], sw_s.at[i], sw_r.at[i], (sibling, band))

    def even_copy(k):
        target = 2 * lax.rem(chip + k, chips)
        return remote(
            video_ref.at[:, :, columns(target)], frames_buf.at[me], a_s.at[k], a_r.at[2 * k + core], (target, band)
        )

    order_b = [2, 1, 3, 0]
    for i in order_b:
        swap_copy(i).start()

    for k in far_first(chips):
        even_copy(k).start()

    @pl.when(core == 1)
    def _():
        even_copy(0).start()

    loads = [
        pltpu.make_async_copy(src, dst, local_sem.at[6 + i])
        for i, (src, dst) in enumerate([(video_ref, video_buf), (split_ref, split_buf), (dual_ref, dual_buf)])
    ]
    for copy in loads:
        copy.start()
    for copy in small[:2]:
        copy.wait()

    def on(frame, band_index):
        inside = (band_index >= 0) & (band_index < bands)
        at = jnp.clip(band_index, 0, bands - 1)
        active = inside & (start_ref[at] <= frame) & (frame < end_ref[at])
        return jnp.where(active, 1.0, 0.0).astype(F32)

    def kept(value, index, count):
        return value * jnp.where((index >= 0) & (index < count), 1.0, 0.0).astype(value.dtype)

    def weighted(pairs):
        total = None
        for value, weight in pairs:
            total = value * weight if total is None else total + value * weight
        return total

    def tb_copy(i, d):
        return remote(
            tb_send.at[i, d + REACH], tb_recv.at[i, REACH - d], tb_s.at[i, d + REACH], tb_r.at[i, REACH - d], row_peer(d)
        )

    def tb_arrival(i, d):
        return remote(tb_send.at[i, d + REACH], tb_recv.at[i, d + REACH], tb_s.at[i, d + REACH], tb_r.at[i, d + REACH], row_peer(d))

    half = block // 4
    for i in order_b:
        own_copies[i].wait()
        swap_copy(i).wait_recv()

        def mix(c, carry):
            part = pl.ds(pl.multiple_of(c * half, half), half)
            mine = [(own_buf[i, f, part].astype(F32), me * local_count + f) for f in range(local_count)]
            others = [(swap_buf[i, f, part].astype(F32), sibling * local_count + f) for f in range(local_count)]
            for d in diagonals:
                total = weighted([(value, on(frame, band + d)) for value, frame in mine + others]).astype(BF16)
                if d == 0:
                    tb_recv[i, REACH, part] = total
                else:
                    tb_send[i, d + REACH, part] = total
            return carry

        lax.fori_loop(0, 4, mix, 0)
        for d in steps:
            tb_copy(i, d).start()

    for copy in small[2:]:
        copy.wait()
    ranks = spans(rank_count, block)
    blocks = spans(DIAGS, block)
    banded(kv_ref, bands_f32, block)
    for r in range(rank_count):
        vert[ranks[r]] = bands_f32[r].astype(BF16)
        for cols in blocks:
            vert_t[cols, ranks[r]] = bands_f32[r, :, cols].T.astype(BF16)
    banded(kh_ref, bands_f32, block)
    for r in range(rank_count):
        for cols in blocks:
            horiz_p[ranks[r], cols] = bands_f32[r, :, cols].T.astype(BF16)
            horiz_q[cols, ranks[r]] = bands_f32[r, :, cols].astype(BF16)

    for copy in loads:
        copy.wait()

    def pull(c, carry):
        part = pl.ds(pl.multiple_of(c * 16, 16), 16)
        for f in range(local_count):
            current = video_buf[f, part].astype(F32)
            apart = current - split_buf[f, part].astype(F32) + dual_buf[f, part].astype(F32)
            base_ref[f, part] = current - tau_step * rho_weight * apart
        return carry

    lax.fori_loop(0, block // 16, pull, 0)

    def add_frames(source, first):
        for d in diagonals:
            total = None if first else sums[d + REACH]
            for f in range(local_count):
                term = frames_buf[source, f].astype(F32) * on(source * local_count + f, band + d)
                total = term if total is None else total + term
            sums[d + REACH] = total

    def even_arrival(k, from_core):
        source = 2 * wrap(chip - k, chips) + from_core
        remote(frames_buf.at[source], frames_buf.at[source], a_s.at[k], a_r.at[2 * k + from_core], (sibling, band)).wait_recv()
        add_frames(source, False)

    def gather_even(low, high):
        def take(q, carry):
            k = wrap(((q + 1) // 2) * (2 * lax.rem(q, 2) - 1), chips)
            even_arrival(k, 0)
            even_arrival(k, 1)
            return carry

        lax.fori_loop(low, high, take, 0)

    def t_copy(d):
        return remote(
            t_send.at[d + REACH], t_recv.at[REACH - d], t_s.at[d + REACH], t_r.at[REACH - d], row_peer(d)
        )

    def t_arrival(d):
        return remote(t_send.at[d + REACH], t_recv.at[d + REACH], t_s.at[d + REACH], t_r.at[d + REACH], row_peer(d))

    def vertical(window_ref, store):
        window = jnp.concatenate([kept(window_ref[d + REACH], band + d, bands) for d in diagonals], axis=0)
        products = dot(vert[...], window, ((1,), (0,))).astype(BF16)
        for r in range(rank_count):
            store[r] = products[ranks[r]]

    def part_copy(i):
        owner = 2 * odd_chip(i) + 1
        k = skew + 2 * i
        return remote(part_send.at[i], part_recv.at[k], part_s.at[i], part_r.at[k], (owner, band))

    own_share = (core == 1) & (skew == 0)

    for position, i in enumerate(order_b):
        for d in steps:
            tb_arrival(i, d).wait_recv()
        vertical(tb_recv.at[i], part_send.at[i])
        if i == 0:

            @pl.when(own_share)
            def _():
                part_recv[0] = part_send[0]

            @pl.when(jnp.logical_not(own_share))
            def _():
                part_copy(0).start()

        else:
            part_copy(i).start()

        @pl.when(core == 0)
        def _():
            if position == 0:
                own_even.wait()
                add_frames(me, True)
                even_arrival(0, 1)
                gather_even(1, 3)
            if position == 1:
                gather_even(3, 5)
            if position == 2:
                gather_even(5, chips)
                for d in steps:
                    t_send[d + REACH] = sums[d + REACH].astype(BF16)
                    t_copy(d).start()
                t_recv[REACH] = sums[REACH].astype(BF16)

    @pl.when(core == 0)
    def _():
        for d in steps:
            t_arrival(d).wait_recv()
        vertical(t_recv, rowed_ref)

    def part_arrival(k):
        remote(part_send.at[0], part_recv.at[k], part_s.at[0], part_r.at[k], (sibling, band)).wait_recv()

    @pl.when(core == 1)
    def _():
        @pl.when(jnp.logical_not(own_share))
        def _():
            part_arrival(0)

        for k in range(1, chips):
            part_arrival(k)
        for r in range(rank_count):
            total = part_recv[0, r].astype(F32)
            for k in range(1, chips):
                total = total + part_recv[k, r].astype(F32)
            rowed_ref[r] = total.astype(BF16)

    def p_copy(d):
        return remote(
            p_send.at[d + REACH], p_recv.at[d + REACH], p_s.at[d + REACH], p_r.at[d + REACH], frame_peer(-d)
        )

    rowed = jnp.concatenate([rowed_ref[r] for r in range(rank_count)], axis=1)
    products = dot(rowed, horiz_p[...], ((1,), (0,)))
    for d in steps:
        p_send[d + REACH] = products[:, blocks[d + REACH]].astype(BF16)
        p_copy(d).start()
    measured = products[:, blocks[REACH]]
    for d in steps:
        p_copy(d).wait_recv()
        measured = measured + kept(p_recv[d + REACH].astype(F32), me + d, frame_devices)
    sensor_copy.wait()
    res_recv[REACH] = (measured - sensor_buf[...]).astype(BF16)

    def r_copy(d):
        return remote(
            res_recv.at[REACH], res_recv.at[d + REACH], r_s.at[d + REACH], r_r.at[d + REACH], frame_peer(d)
        )

    for d in steps:
        r_copy(d).start()
    for d in steps:
        r_copy(d).wait_recv()
    pieces = jnp.concatenate([kept(res_recv[d + REACH], me - d, frame_devices) for d in diagonals], axis=1)
    products = dot(pieces, horiz_q[...], ((1,), (0,))).astype(BF16)
    for r in range(rank_count):
        spread[r] = products[:, ranks[r]]

    def q_copy(k):
        target = 2 * wrap(chip - k, chips) + lax.rem(chip, 2)
        return remote(spread, q_recv.at[k // 2], q_s.at[k], q_r.at[k // 2], (target, band))

    @pl.when(core == 1)
    def _():
        @pl.when(own_share)
        def _():
            q_recv[0] = spread[...]

        @pl.when(jnp.logical_not(own_share))
        def _():
            q_copy(0).start()

        for k in [1, 7, 2, 6, 3, 5, 4]:
            q_copy(k).start()

    def adjoint(tile_ref, store, keep):
        tile = tile_ref[...].reshape(rank_count * block, slice_cols)
        products = dot(vert_t[...], tile, ((1,), (0,))).astype(BF16)
        for d in diagonals:
            target = keep if d == 0 else store
            target[d + REACH] = products[blocks[d + REACH]]

    def h_copy(d):
        return remote(
            h_send.at[d + REACH], h_recv.at[d + REACH], h_s.at[d + REACH], h_r.at[d + REACH], row_peer(d)
        )

    @pl.when(core == 0)
    def _():
        adjoint(spread, h_send, h_recv)
        for d in steps:
            h_copy(d).start()

    def hb_copy(i, d):
        return remote(
            hb_send.at[i, d + REACH], hb_recv.at[i, d + REACH], hb_s.at[i, d + REACH], hb_r.at[i, d + REACH], row_peer(d)
        )

    def gradient(sources_ref, frame, part):
        return weighted(
            [(sources_ref[d + REACH, part].astype(F32), on(frame, band - d)) for d in diagonals]
        ).astype(BF16)

    def g_copy(k):
        target = wrap(me + k, frame_devices)
        distance = wrap(target // 2 - chip, chips)
        return remote(
            g_send.at[target], grad_ref.at[:, :, columns(me)], g_s.at[k], g_r.at[distance], (target, band)
        )

    def give(q, carry):
        k = chips + ((q + 1) // 2) * (2 * lax.rem(q, 2) - 1)
        target = wrap(me + k, frame_devices)
        for f in range(local_count):
            g_send[target, f] = gradient(h_recv, target * local_count + f, slice(None))
        g_copy(k).start()
        return carry

    def q_arrival(i):
        remote(spread, q_recv.at[i], q_s.at[0], q_r.at[i], (sibling, band)).wait_recv()

    for position, i in enumerate([0, 3, 1, 2]):
        if i == 0:

            @pl.when(jnp.logical_not(own_share))
            def _():
                q_arrival(0)

        else:
            q_arrival(i)
        adjoint(q_recv.at[i], hb_send.at[i], hb_recv.at[i])
        for d in steps:
            hb_copy(i, d).start()
        if position == 0:

            @pl.when(core == 0)
            def _():
                for d in steps:
                    h_copy(d).wait_recv()
                lax.fori_loop(0, frame_devices - 1, give, 0)
                for f in range(local_count):
                    grad_ref[f, :, columns(me)] = gradient(h_recv, me * local_count + f, slice(None))

    def gb_copy(i):
        return remote(
            gb_send.at[i], grad_ref.at[:, :, columns(2 * odd_chip(i) + 1)], gb_s.at[i], gb_r.at[i], (sibling, band)
        )

    def gb_arrival(i):
        index = 2 * lax.rem(chip + 1 - skew + 2 * i, chips) + 1
        return remote(gb_send.at[i], grad_ref.at[:, :, columns(index)], gb_s.at[i], gb_r.at[i], (sibling, band))

    for i in [0, 3, 1, 2]:
        for d in steps:
            hb_copy(i, d).wait_recv()
        for f in range(local_count):
            gb_send[i, f] = gradient(hb_recv.at[i], sibling * local_count + f, slice(None))
        gb_copy(i).start()
        for f in range(local_count):
            grad_ref[f, :, columns(2 * odd_chip(i) + 1)] = gradient(
                hb_recv.at[i], me * local_count + f, slice(None)
            )

    def g_arrival(k):
        index = 2 * wrap(chip - k, chips)
        remote(g_send.at[0], grad_ref.at[:, :, columns(index)], g_s.at[0], g_r.at[k], (sibling, band)).wait_recv()

    for k in range(1, chips):
        g_arrival(k)

    @pl.when(core == 1)
    def _():
        g_arrival(0)
        even_copy(0).wait_send()
        for k in range(1, chips):
            q_copy(k).wait_send()

        @pl.when(jnp.logical_not(own_share))
        def _():
            q_copy(0).wait_send()

    @pl.when(core == 0)
    def _():
        def depart(k, carry):
            g_copy(k).wait_send()
            return carry

        lax.fori_loop(1, frame_devices, depart, 0)
        for d in steps:
            t_copy(d).wait_send()
            h_copy(d).wait_send()

    @pl.when(jnp.logical_not(own_share))
    def _():
        part_copy(0).wait_send()

    for k in range(1, chips):
        even_copy(k).wait_send()
    for i in range(shares):
        gb_arrival(i).wait_recv()
        gb_copy(i).wait_send()
        swap_copy(i).wait_send()
        if i > 0:
            part_copy(i).wait_send()
        for d in steps:
            tb_copy(i, d).wait_send()
            hb_copy(i, d).wait_send()
    for d in steps:
        p_copy(d).wait_send()
        r_copy(d).wait_send()


def per_device(
    video_frames, split_frames, dual_frames, sensor_image, kernel_vertical, kernel_horizontal, shutter_start, shutter_end
):
    local_count, block, width = video_frames.shape
    rank_count, taps = kernel_vertical.shape
    frame_devices = lax.axis_size("frame")
    slice_cols = width // frame_devices
    chips = frame_devices // 2
    shares = chips // 2
    hbm = pl.BlockSpec(memory_space=pltpu.HBM)
    dma = pltpu.SemaphoreType.DMA
    tile = (block, slice_cols)
    operands = (shutter_start, shutter_end, video_frames, sensor_image, kernel_vertical, kernel_horizontal, split_frames, dual_frames)
    gradient, base = pl.pallas_call(
        kernel,
        out_shape=[jax.ShapeDtypeStruct((local_count, block, width), kind) for kind in (BF16, F32)],
        in_specs=[hbm] * 8,
        out_specs=[pl.BlockSpec(memory_space=pltpu.VMEM)] * 2,
        scratch_shapes=[pltpu.VMEM((local_count, block, width), BF16)] * 3
        + [
            pltpu.SMEM(shutter_start.shape, jnp.int32),
            pltpu.SMEM(shutter_end.shape, jnp.int32),
            pltpu.VMEM((rank_count, taps), BF16),
            pltpu.VMEM((rank_count, taps), BF16),
            pltpu.VMEM(tile, F32),
            pltpu.VMEM((rank_count, block, taps + block), F32),
            pltpu.VMEM((rank_count * block, taps + block), BF16),
            pltpu.VMEM((taps + block, rank_count * block), BF16),
            pltpu.VMEM((rank_count * block, taps + block), BF16),
            pltpu.VMEM((taps + block, rank_count * block), BF16),
            pltpu.VMEM((DIAGS,) + tile, F32),
        ]
        + [
            pltpu.VMEM(lead + tile, BF16)
            for lead in [
                (rank_count,), (rank_count,),
                (frame_devices, local_count), (shares, local_count), (shares, local_count),
                (shares, DIAGS), (shares, DIAGS), (shares, rank_count), (chips, rank_count),
                (DIAGS,), (DIAGS,), (DIAGS,), (DIAGS,), (DIAGS,), (DIAGS,), (DIAGS,),
                (shares, rank_count), (shares, DIAGS), (shares, DIAGS),
                (frame_devices, local_count), (shares, local_count),
            ]
        ]
        + [
            dma(count)
            for count in [
                (9,), (shares,), (shares,), (shares,), (chips,), (frame_devices,),
                (shares, DIAGS), (shares, DIAGS), (shares,), (chips,), (DIAGS,), (DIAGS,),
                (DIAGS,), (DIAGS,), (DIAGS,), (DIAGS,), (DIAGS,), (DIAGS,), (chips,), (shares,),
                (shares, DIAGS), (shares, DIAGS), (frame_devices,), (chips,), (shares,), (shares,),
            ]
        ],
        compiler_params=pltpu.CompilerParams(
            collective_id=0, has_side_effects=True, vmem_limit_bytes=32 << 20
        ),
        name="blur_and_adjoint",
    )(*[pltpu.with_memory_space_constraint(x, pltpu.HBM) for x in operands])
    moved_frames = base - tau_step * gradient.astype(F32)
    shifted = moved_frames + dual_frames.astype(F32)
    clamped = jnp.maximum(shifted, 0.0)
    return (
        moved_frames.astype(BF16),
        clamped.astype(BF16),
        (shifted - clamped).astype(BF16),
    )


def solution(mesh):
    frames = P("frame", "row", None)
    return jax.shard_map(
        per_device,
        mesh=mesh,
        in_specs=(frames, frames, frames, P("row", None), P(), P(), P(), P()),
        out_specs=(frames, frames, frames),
        check_vma=False,
    )
```

```python
import functools

import jax
import jax.numpy as jnp
from jax import lax
from jax.experimental import pallas as pl
from jax.experimental.pallas import tpu as pltpu
from jax.sharding import PartitionSpec as P

MESH = pl.DeviceIdType.MESH
tau_step = 0.1
rho_weight = 2.0
REACH = 3
DIAGS = 2 * REACH + 1
F32 = jnp.float32
BF16 = jnp.bfloat16


def dot(a, b, contract):
    return lax.dot_general(a, b, (contract, ((), ())), preferred_element_type=F32)


def far_first(count):
    return sorted(range(1, count), key=lambda k: -min(k, count - k))


def wrap(index, count):
    return lax.rem(index + count, count)


def banded(kernel_ref, scratch, block):
    rank_count, taps = kernel_ref.shape
    padded = jnp.concatenate(
        [kernel_ref[...].astype(F32), jnp.zeros((rank_count, block), F32)], axis=1
    )
    for r in range(rank_count):
        rows = jnp.broadcast_to(padded[r : r + 1], (block, taps + block))
        scratch[r] = pltpu.roll(rows, 0, 1, stride=1, stride_axis=0)


def spans(count, block):
    return [slice(i * block, (i + 1) * block) for i in range(count)]


def kernel(
    start_hbm, end_hbm, video_ref, sensor_ref, kv_hbm, kh_hbm, split_ref, dual_ref, grad_ref, base_ref,
    video_buf, split_buf, dual_buf,
    start_ref, end_ref, kv_ref, kh_ref, sensor_buf, bands_f32, vert, vert_t, horiz_p, horiz_q, sums, rowed_ref, spread,
    frames_buf, own_buf, swap_buf, tb_send, tb_recv, part_send, part_recv, t_send, t_recv,
    p_send, p_recv, res_recv, h_send, h_recv, q_recv, hb_send, hb_recv, g_send, gb_send,
    local_sem, own_sem, sw_s, sw_r, a_s, a_r, tb_s, tb_r, part_s, part_r, t_s, t_r,
    p_s, p_r, r_s, r_r, h_s, h_r, q_s, q_r, hb_s, hb_r, g_s, g_r, gb_s, gb_r,
):
    frame_devices, local_count, block, slice_cols = frames_buf.shape
    chips = frame_devices // 2
    shares = chips // 2
    bands = start_ref.shape[0]
    rank_count = kv_ref.shape[0]
    me = lax.axis_index("frame")
    band = lax.axis_index("row")
    chip = me // 2
    core = lax.rem(me, 2)
    sibling = me + 1 - 2 * core
    skew = lax.rem(core + chip, 2)
    steps = [3, -3, 2, -2, 1, -1]
    diagonals = range(-REACH, REACH + 1)

    def frame_peer(d):
        return (wrap(me + d, frame_devices), band)

    def row_peer(d):
        return (me, wrap(band + d, bands))

    def columns(index):
        return pl.ds(pl.multiple_of(index * slice_cols, slice_cols), slice_cols)

    def odd_chip(i):
        return lax.rem(chip + skew + 2 * i, chips)

    def remote(src, dst, send_sem, recv_sem, target):
        return pltpu.make_async_remote_copy(
            src_ref=src, dst_ref=dst, send_sem=send_sem, recv_sem=recv_sem,
            device_id=target, device_id_type=MESH,
        )

    small = [
        pltpu.make_async_copy(src, dst, local_sem.at[2 + i])
        for i, (src, dst) in enumerate(
            [(start_hbm, start_ref), (end_hbm, end_ref), (kv_hbm, kv_ref), (kh_hbm, kh_ref)]
        )
    ]
    for copy in small:
        copy.start()
    own_copies = [
        pltpu.make_async_copy(video_ref.at[:, :, columns(2 * odd_chip(i) + 1)], own_buf.at[i], own_sem.at[i])
        for i in range(shares)
    ]
    for copy in own_copies:
        copy.start()
    own_even = pltpu.make_async_copy(video_ref.at[:, :, columns(2 * chip)], frames_buf.at[me], local_sem.at[0])
    sensor_copy = pltpu.make_async_copy(sensor_ref.at[:, columns(me)], sensor_buf, local_sem.at[1])
    sensor_copy.start()

    @pl.when(core == 0)
    def _():
        own_even.start()

    barrier = pltpu.get_barrier_semaphore()

    def greet(k, carry):
        pl.semaphore_signal(barrier, inc=1, device_id=frame_peer(k), device_id_type=MESH)
        return carry

    for k in far_first(frame_devices):
        greet(k, 0)
    for d in steps:
        pl.semaphore_signal(barrier, inc=1, device_id=row_peer(d), device_id_type=MESH)
    pl.semaphore_wait(barrier, frame_devices - 1 + len(steps))

    def swap_copy(i):
        index = 2 * lax.rem(chip + 1 - skew + 2 * i, chips) + 1
        return remote(video_ref.at[:, :, columns(index)], swap_buf.at[i], sw_s.at[i], sw_r.at[i], (sibling, band))

    def even_copy(k):
        target = 2 * lax.rem(chip + k, chips)
        return remote(
            video_ref.at[:, :, columns(target)], frames_buf.at[me], a_s.at[k], a_r.at[2 * k + core], (target, band)
        )

    order_b = [2, 1, 3, 0]
    for i in order_b:
        swap_copy(i).start()

    for k in far_first(chips):
        even_copy(k).start()

    @pl.when(core == 1)
    def _():
        even_copy(0).start()

    loads = [
        pltpu.make_async_copy(src, dst, local_sem.at[6 + i])
        for i, (src, dst) in enumerate([(video_ref, video_buf), (split_ref, split_buf), (dual_ref, dual_buf)])
    ]
    for copy in loads:
        copy.start()
    for copy in small[:2]:
        copy.wait()

    def on(frame, band_index):
        inside = (band_index >= 0) & (band_index < bands)
        at = jnp.clip(band_index, 0, bands - 1)
        active = inside & (start_ref[at] <= frame) & (frame < end_ref[at])
        return jnp.where(active, 1.0, 0.0).astype(F32)

    def kept(value, index, count):
        return value * jnp.where((index >= 0) & (index < count), 1.0, 0.0).astype(value.dtype)

    def weighted(pairs):
        total = None
        for value, weight in pairs:
            total = value * weight if total is None else total + value * weight
        return total

    def tb_copy(i, d):
        return remote(
            tb_send.at[i, d + REACH], tb_recv.at[i, REACH - d], tb_s.at[i, d + REACH], tb_r.at[i, REACH - d], row_peer(d)
        )

    def tb_arrival(i, d):
        return remote(tb_send.at[i, d + REACH], tb_recv.at[i, d + REACH], tb_s.at[i, d + REACH], tb_r.at[i, d + REACH], row_peer(d))

    half = block // 4
    for i in order_b:
        own_copies[i].wait()
        swap_copy(i).wait_recv()

        def mix(c, carry):
            part = pl.ds(pl.multiple_of(c * half, half), half)
            mine = [(own_buf[i, f, part].astype(F32), me * local_count + f) for f in range(local_count)]
            others = [(swap_buf[i, f, part].astype(F32), sibling * local_count + f) for f in range(local_count)]
            for d in diagonals:
                total = weighted([(value, on(frame, band + d)) for value, frame in mine + others]).astype(BF16)
                if d == 0:
                    tb_recv[i, REACH, part] = total
                else:
                    tb_send[i, d + REACH, part] = total
            return carry

        lax.fori_loop(0, 4, mix, 0)
        for d in steps:
            tb_copy(i, d).start()

    for copy in small[2:]:
        copy.wait()
    ranks = spans(rank_count, block)
    blocks = spans(DIAGS, block)
    banded(kv_ref, bands_f32, block)
    for r in range(rank_count):
        vert[ranks[r]] = bands_f32[r].astype(BF16)
        for cols in blocks:
            vert_t[cols, ranks[r]] = bands_f32[r, :, cols].T.astype(BF16)
    banded(kh_ref, bands_f32, block)
    for r in range(rank_count):
        for cols in blocks:
            horiz_p[ranks[r], cols] = bands_f32[r, :, cols].T.astype(BF16)
            horiz_q[cols, ranks[r]] = bands_f32[r, :, cols].astype(BF16)

    for copy in loads:
        copy.wait()

    def pull(c, carry):
        part = pl.ds(pl.multiple_of(c * 16, 16), 16)
        for f in range(local_count):
            current = video_buf[f, part].astype(F32)
            apart = current - split_buf[f, part].astype(F32) + dual_buf[f, part].astype(F32)
            base_ref[f, part] = current - tau_step * rho_weight * apart
        return carry

    lax.fori_loop(0, block // 16, pull, 0)

    def add_frames(source, first):
        for d in diagonals:
            total = None if first else sums[d + REACH]
            for f in range(local_count):
                term = frames_buf[source, f].astype(F32) * on(source * local_count + f, band + d)
                total = term if total is None else total + term
            sums[d + REACH] = total

    def even_arrival(k, from_core):
        source = 2 * wrap(chip - k, chips) + from_core
        remote(frames_buf.at[source], frames_buf.at[source], a_s.at[k], a_r.at[2 * k + from_core], (sibling, band)).wait_recv()
        add_frames(source, False)

    def gather_even(low, high):
        def take(q, carry):
            k = wrap(((q + 1) // 2) * (2 * lax.rem(q, 2) - 1), chips)
            even_arrival(k, 0)
            even_arrival(k, 1)
            return carry

        lax.fori_loop(low, high, take, 0)

    def t_copy(d):
        return remote(
            t_send.at[d + REACH], t_recv.at[REACH - d], t_s.at[d + REACH], t_r.at[REACH - d], row_peer(d)
        )

    def t_arrival(d):
        return remote(t_send.at[d + REACH], t_recv.at[d + REACH], t_s.at[d + REACH], t_r.at[d + REACH], row_peer(d))

    def vertical(window_ref, store):
        window = jnp.concatenate([kept(window_ref[d + REACH], band + d, bands) for d in diagonals], axis=0)
        products = dot(vert[...], window, ((1,), (0,))).astype(BF16)
        for r in range(rank_count):
            store[r] = products[ranks[r]]

    def part_copy(i):
        owner = 2 * odd_chip(i) + 1
        k = skew + 2 * i
        return remote(part_send.at[i], part_recv.at[k], part_s.at[i], part_r.at[k], (owner, band))

    own_share = (core == 1) & (skew == 0)

    for position, i in enumerate(order_b):
        for d in steps:
            tb_arrival(i, d).wait_recv()
        vertical(tb_recv.at[i], part_send.at[i])
        if i == 0:

            @pl.when(own_share)
            def _():
                part_recv[0] = part_send[0]

            @pl.when(jnp.logical_not(own_share))
            def _():
                part_copy(0).start()

        else:
            part_copy(i).start()

        @pl.when(core == 0)
        def _():
            if position == 0:
                own_even.wait()
                add_frames(me, True)
                even_arrival(0, 1)
                gather_even(1, 3)
            if position == 1:
                gather_even(3, 5)
            if position == 2:
                gather_even(5, chips)
                for d in steps:
                    t_send[d + REACH] = sums[d + REACH].astype(BF16)
                    t_copy(d).start()
                t_recv[REACH] = sums[REACH].astype(BF16)

    @pl.when(core == 0)
    def _():
        for d in steps:
            t_arrival(d).wait_recv()
        vertical(t_recv, rowed_ref)

    def part_arrival(k):
        remote(part_send.at[0], part_recv.at[k], part_s.at[0], part_r.at[k], (sibling, band)).wait_recv()

    @pl.when(core == 1)
    def _():
        @pl.when(jnp.logical_not(own_share))
        def _():
            part_arrival(0)

        for k in range(1, chips):
            part_arrival(k)
        for r in range(rank_count):
            total = part_recv[0, r].astype(F32)
            for k in range(1, chips):
                total = total + part_recv[k, r].astype(F32)
            rowed_ref[r] = total.astype(BF16)

    def p_copy(d):
        return remote(
            p_send.at[d + REACH], p_recv.at[d + REACH], p_s.at[d + REACH], p_r.at[d + REACH], frame_peer(-d)
        )

    rowed = jnp.concatenate([rowed_ref[r] for r in range(rank_count)], axis=1)
    products = dot(rowed, horiz_p[...], ((1,), (0,)))
    for d in steps:
        p_send[d + REACH] = products[:, blocks[d + REACH]].astype(BF16)
        p_copy(d).start()
    measured = products[:, blocks[REACH]]
    sensor_copy.wait()
    measured = measured - sensor_buf[...]
    for d in reversed(steps):
        p_copy(d).wait_recv()
        measured = measured + kept(p_recv[d + REACH].astype(F32), me + d, frame_devices)
    res_recv[REACH] = measured.astype(BF16)

    def r_copy(d):
        return remote(
            res_recv.at[REACH], res_recv.at[d + REACH], r_s.at[d + REACH], r_r.at[d + REACH], frame_peer(d)
        )

    for d in steps:
        r_copy(d).start()
    for d in steps:
        r_copy(d).wait_recv()
    pieces = jnp.concatenate([kept(res_recv[d + REACH], me - d, frame_devices) for d in diagonals], axis=1)
    products = dot(pieces, horiz_q[...], ((1,), (0,))).astype(BF16)
    for r in range(rank_count):
        spread[r] = products[:, ranks[r]]

    def q_copy(k):
        target = 2 * wrap(chip - k, chips) + lax.rem(chip, 2)
        return remote(spread, q_recv.at[k // 2], q_s.at[k], q_r.at[k // 2], (target, band))

    @pl.when(core == 1)
    def _():
        @pl.when(own_share)
        def _():
            q_recv[0] = spread[...]

        @pl.when(jnp.logical_not(own_share))
        def _():
            q_copy(0).start()

        for k in [1, 7, 2, 6, 3, 5, 4]:
            q_copy(k).start()

    def adjoint(tile_ref, store, keep):
        tile = tile_ref[...].reshape(rank_count * block, slice_cols)
        products = dot(vert_t[...], tile, ((1,), (0,))).astype(BF16)
        for d in diagonals:
            target = keep if d == 0 else store
            target[d + REACH] = products[blocks[d + REACH]]

    def h_copy(d):
        return remote(
            h_send.at[d + REACH], h_recv.at[d + REACH], h_s.at[d + REACH], h_r.at[d + REACH], row_peer(d)
        )

    @pl.when(core == 0)
    def _():
        adjoint(spread, h_send, h_recv)
        for d in steps:
            h_copy(d).start()

    def hb_copy(i, d):
        return remote(
            hb_send.at[i, d + REACH], hb_recv.at[i, d + REACH], hb_s.at[i, d + REACH], hb_r.at[i, d + REACH], row_peer(d)
        )

    def gradient(sources_ref, frame, part):
        return weighted(
            [(sources_ref[d + REACH, part].astype(F32), on(frame, band - d)) for d in diagonals]
        ).astype(BF16)

    def g_copy(k):
        target = wrap(me + k, frame_devices)
        distance = wrap(target // 2 - chip, chips)
        return remote(
            g_send.at[target], grad_ref.at[:, :, columns(me)], g_s.at[k], g_r.at[distance], (target, band)
        )

    def give(q, carry):
        k = chips + ((q + 1) // 2) * (2 * lax.rem(q, 2) - 1)
        target = wrap(me + k, frame_devices)
        for f in range(local_count):
            g_send[target, f] = gradient(h_recv, target * local_count + f, slice(None))
        g_copy(k).start()
        return carry

    def q_arrival(i):
        remote(spread, q_recv.at[i], q_s.at[0], q_r.at[i], (sibling, band)).wait_recv()

    for position, i in enumerate([0, 3, 1, 2]):
        if i == 0:

            @pl.when(jnp.logical_not(own_share))
            def _():
                q_arrival(0)

        else:
            q_arrival(i)
        adjoint(q_recv.at[i], hb_send.at[i], hb_recv.at[i])
        for d in steps:
            hb_copy(i, d).start()
        if position == 0:

            @pl.when(core == 0)
            def _():
                for d in steps:
                    h_copy(d).wait_recv()
                lax.fori_loop(0, frame_devices - 1, give, 0)
                for f in range(local_count):
                    grad_ref[f, :, columns(me)] = gradient(h_recv, me * local_count + f, slice(None))

    def gb_copy(i):
        return remote(
            gb_send.at[i], grad_ref.at[:, :, columns(2 * odd_chip(i) + 1)], gb_s.at[i], gb_r.at[i], (sibling, band)
        )

    def gb_arrival(i):
        index = 2 * lax.rem(chip + 1 - skew + 2 * i, chips) + 1
        return remote(gb_send.at[i], grad_ref.at[:, :, columns(index)], gb_s.at[i], gb_r.at[i], (sibling, band))

    for i in [0, 3, 1, 2]:
        for d in steps:
            hb_copy(i, d).wait_recv()
        for f in range(local_count):
            gb_send[i, f] = gradient(hb_recv.at[i], sibling * local_count + f, slice(None))
        gb_copy(i).start()
        for f in range(local_count):
            grad_ref[f, :, columns(2 * odd_chip(i) + 1)] = gradient(
                hb_recv.at[i], me * local_count + f, slice(None)
            )

    def g_arrival(k):
        index = 2 * wrap(chip - k, chips)
        remote(g_send.at[0], grad_ref.at[:, :, columns(index)], g_s.at[0], g_r.at[k], (sibling, band)).wait_recv()

    for k in range(1, chips):
        g_arrival(k)

    @pl.when(core == 1)
    def _():
        g_arrival(0)
        even_copy(0).wait_send()
        for k in range(1, chips):
            q_copy(k).wait_send()

        @pl.when(jnp.logical_not(own_share))
        def _():
            q_copy(0).wait_send()

    @pl.when(core == 0)
    def _():
        def depart(k, carry):
            g_copy(k).wait_send()
            return carry

        lax.fori_loop(1, frame_devices, depart, 0)
        for d in steps:
            t_copy(d).wait_send()
            h_copy(d).wait_send()

    @pl.when(jnp.logical_not(own_share))
    def _():
        part_copy(0).wait_send()

    for k in range(1, chips):
        even_copy(k).wait_send()
    for i in range(shares):
        gb_arrival(i).wait_recv()
        gb_copy(i).wait_send()
        swap_copy(i).wait_send()
        if i > 0:
            part_copy(i).wait_send()
        for d in steps:
            tb_copy(i, d).wait_send()
            hb_copy(i, d).wait_send()
    for d in steps:
        p_copy(d).wait_send()
        r_copy(d).wait_send()


def per_device(
    video_frames, split_frames, dual_frames, sensor_image, kernel_vertical, kernel_horizontal, shutter_start, shutter_end
):
    local_count, block, width = video_frames.shape
    rank_count, taps = kernel_vertical.shape
    frame_devices = lax.axis_size("frame")
    slice_cols = width // frame_devices
    chips = frame_devices // 2
    shares = chips // 2
    hbm = pl.BlockSpec(memory_space=pltpu.HBM)
    dma = pltpu.SemaphoreType.DMA
    tile = (block, slice_cols)
    operands = (shutter_start, shutter_end, video_frames, sensor_image, kernel_vertical, kernel_horizontal, split_frames, dual_frames)
    gradient, base = pl.pallas_call(
        kernel,
        out_shape=[jax.ShapeDtypeStruct((local_count, block, width), kind) for kind in (BF16, F32)],
        in_specs=[hbm] * 8,
        out_specs=[pl.BlockSpec(memory_space=pltpu.VMEM)] * 2,
        scratch_shapes=[pltpu.VMEM((local_count, block, width), BF16)] * 3
        + [
            pltpu.SMEM(shutter_start.shape, jnp.int32),
            pltpu.SMEM(shutter_end.shape, jnp.int32),
            pltpu.VMEM((rank_count, taps), BF16),
            pltpu.VMEM((rank_count, taps), BF16),
            pltpu.VMEM(tile, F32),
            pltpu.VMEM((rank_count, block, taps + block), F32),
            pltpu.VMEM((rank_count * block, taps + block), BF16),
            pltpu.VMEM((taps + block, rank_count * block), BF16),
            pltpu.VMEM((rank_count * block, taps + block), BF16),
            pltpu.VMEM((taps + block, rank_count * block), BF16),
            pltpu.VMEM((DIAGS,) + tile, F32),
        ]
        + [
            pltpu.VMEM(lead + tile, BF16)
            for lead in [
                (rank_count,), (rank_count,),
                (frame_devices, local_count), (shares, local_count), (shares, local_count),
                (shares, DIAGS), (shares, DIAGS), (shares, rank_count), (chips, rank_count),
                (DIAGS,), (DIAGS,), (DIAGS,), (DIAGS,), (DIAGS,), (DIAGS,), (DIAGS,),
                (shares, rank_count), (shares, DIAGS), (shares, DIAGS),
                (frame_devices, local_count), (shares, local_count),
            ]
        ]
        + [
            dma(count)
            for count in [
                (9,), (shares,), (shares,), (shares,), (chips,), (frame_devices,),
                (shares, DIAGS), (shares, DIAGS), (shares,), (chips,), (DIAGS,), (DIAGS,),
                (DIAGS,), (DIAGS,), (DIAGS,), (DIAGS,), (DIAGS,), (DIAGS,), (chips,), (shares,),
                (shares, DIAGS), (shares, DIAGS), (frame_devices,), (chips,), (shares,), (shares,),
            ]
        ],
        compiler_params=pltpu.CompilerParams(
            collective_id=0, has_side_effects=True, vmem_limit_bytes=32 << 20
        ),
        name="blur_and_adjoint",
    )(*[pltpu.with_memory_space_constraint(x, pltpu.HBM) for x in operands])
    moved_frames = base - tau_step * gradient.astype(F32)
    shifted = moved_frames + dual_frames.astype(F32)
    clamped = jnp.maximum(shifted, 0.0)
    return (
        moved_frames.astype(BF16),
        clamped.astype(BF16),
        (shifted - clamped).astype(BF16),
    )


def solution(mesh):
    frames = P("frame", "row", None)
    return jax.shard_map(
        per_device,
        mesh=mesh,
        in_specs=(frames, frames, frames, P("row", None), P(), P(), P(), P()),
        out_specs=(frames, frames, frames),
        check_vma=False,
    )
```
